256 devices in a mesh: cell: 64 (over x, z, core), blk: 4 (over y).
Axes of the slice: x: 4, y: 4, z: 8, core: 2. Of those that a mesh axis runs over, the one named last changes fastest.
Arguments:
- velocity_modes: bfloat16 [8, 3, 2, 256, 256, 128], P('blk', None, None, None, 'cell'), may hold values from -6 to 6
- block_list: int32 [2, 2], replicated, may hold values from 0 to 2, as said below
- counts: int32 [2], replicated, may hold values from 1 to 64, as said below
Outputs:
- transfer: float32 [192, 256, 128], P('blk', 'cell')
- triad_sums: float32 [2, 64, 64], replicated
The draws below stay inside these ranges and needn't reach their ends.
Inputs may be any that keep to these rules, and one draw needn't show every extreme that they name: `block_list`: each row (K, L) holds two frequency block numbers with K + L <= 2; no row appears twice. counts[n] offsets 0 .. counts[n] - 1 of block L are live; some listed pair has all 64 offsets live in every draw.
All inputs are finite; a program needn't handle non-finite values.
Results may differ from the reference program's by a relative error of at most 0.0003.
Values may be sent and summed in bfloat16 or wider, within the bound.
A program may use at most 128 MiB of HBM per device.

```python
import math
import jax
import jax.numpy as jnp
import numpy as np
from jax import lax

F = 256
FBLK = 64
NLIST = 2
CY = 8
CZ = 16
NFB = 4
KF = 192
WELCH = 8
NX = 256
YZ = 128


def extreme_pairs():
    return jnp.asarray(np.array([(NFB - 2, 0), (0, NFB - 2)], dtype=np.int32))


def other_pairs():
    listed = [(donor_block, source_block) for donor_block in range(NFB - 1) for source_block in range(NFB - 1) if donor_block + source_block <= NFB - 2 and (not (donor_block == NFB - 2 and source_block == 0)) and (not (donor_block == 0 and source_block == NFB - 2))]
    return jnp.asarray(np.array(listed, dtype=np.int32).reshape(-1, 2))


def draw_block_list(key, part):
    extremes = extreme_pairs()
    others = other_pairs()
    pick = jax.random.randint(jax.random.fold_in(key, 7), (), 0, 2)
    first_row = jnp.take(extremes, pick, axis=0)[None, :]
    order = jax.random.permutation(jax.random.fold_in(key, 3), others.shape[0])[:NLIST - 1]
    stacked = jnp.concatenate([first_row, jnp.take(others, order, axis=0)], axis=0)
    shuffle = jax.random.permutation(jax.random.fold_in(key, 13), NLIST)
    return jnp.take(stacked, shuffle, axis=0).astype(jnp.int32)


def draw_counts(key, part):
    drawn = jax.random.randint(jax.random.fold_in(key, 5), (NLIST,), 1, FBLK + 1)
    chosen = jax.random.randint(jax.random.fold_in(key, 11), (), 0, NLIST)
    return jnp.where(jnp.arange(NLIST) == chosen, FBLK, drawn).astype(jnp.int32)


def shard_levels(own_key, extent, split, low, top_value):
    factor_of, own = 1.0, jax.random.fold_in(own_key, 6)
    for axis_at, blocks in split:
        steps = jnp.exp(jax.random.uniform(jax.random.fold_in(own, axis_at), (blocks,), jnp.float32, low / len(split), top_value / len(split)))
        factor_of = factor_of * jnp.repeat(steps, extent[axis_at] // blocks).reshape([-1 if axis == axis_at else 1 for axis in range(len(extent))])
    return factor_of


def gaussian(stream_key, extent, deviation, reach, pieces=(), kind=jnp.bfloat16):
    result = deviation * jax.random.normal(stream_key, extent, jnp.float32)
    if pieces:
        result = result * shard_levels(stream_key, extent, pieces, -0.22, 0.18)
    return jnp.clip(result, -reach, reach).astype(kind)


def setup_inputs(seed: int = 0) -> dict:
    streams_of = jax.random.split(jax.random.key(seed), 4)
    return {
        "velocity_modes": gaussian(streams_of[0], (WELCH, 3, 2, F, NX, YZ), 1.0, 6.0, ((0, 4), (4, 64))),
        "block_list": draw_block_list(jax.random.fold_in(streams_of[3], 71), 0),
        "counts": draw_counts(jax.random.fold_in(streams_of[3], 71), 0),
    }


def spatial_slopes(field_values):
    padded = jnp.pad(field_values, [(0, 0)] * (field_values.ndim - 3) + [(1, 1)] * 3)
    slope_first = (padded[..., 2:, 1:-1, 1:-1] - padded[..., :-2, 1:-1, 1:-1]) * 0.5
    slope_second = (padded[..., 1:-1, 2:, 1:-1] - padded[..., 1:-1, :-2, 1:-1]) * 0.5
    slope_third = (padded[..., 1:-1, 1:-1, 2:] - padded[..., 1:-1, 1:-1, :-2]) * 0.5
    return (slope_first, slope_second, slope_third)

def triad_density(donor_modes, slopes, receiver):
    accumulated = 0.0
    for component in range(3):
        real_sum = 0.0
        imag_sum = 0.0
        for direction in range(3):
            grad_real = slopes[direction][:, component, 0][:, None]
            grad_imag = slopes[direction][:, component, 1][:, None]
            real_sum = real_sum + donor_modes[:, direction, 0] * grad_real - donor_modes[:, direction, 1] * grad_imag
            imag_sum = imag_sum + donor_modes[:, direction, 0] * grad_imag + donor_modes[:, direction, 1] * grad_real
        accumulated = accumulated + receiver[:, component, 0] * real_sum + receiver[:, component, 1] * imag_sum
    return -lax.optimization_barrier(jnp.sum(accumulated, axis=0))

def reference(velocity_modes, block_list, counts):
    scale_field = 0.25 / math.sqrt(WELCH * FBLK)
    scale_triad = 0.25 / math.sqrt(WELCH * NX * YZ)
    transfer = jnp.zeros((KF, NX * YZ), jnp.float32)
    totals_list = []
    for listed in range(NLIST):
        start_k = (block_list[listed, 0] * FBLK).astype(jnp.int32)
        start_l = (block_list[listed, 1] * FBLK).astype(jnp.int32)
        live_count = counts[listed]
        donor_modes = lax.dynamic_slice_in_dim(velocity_modes, start_k, FBLK, 3).astype(jnp.float32)
        donor_modes = donor_modes.reshape(WELCH, 3, 2, FBLK, NX * YZ)

        def one_offset(running, offset):
            frequency = (start_l + offset).astype(jnp.int32)
            single = lax.dynamic_slice_in_dim(velocity_modes, frequency, 1, 3)[:, :, :, 0].astype(jnp.float32)
            slopes = spatial_slopes(single.reshape(WELCH, 3, 2, NX, CY, CZ))
            slopes = tuple((slope.reshape(WELCH, 3, 2, NX * YZ) for slope in slopes))
            receiver = lax.dynamic_slice_in_dim(velocity_modes, (start_k + frequency).astype(jnp.int32), FBLK, 3)
            receiver = receiver.astype(jnp.float32).reshape(WELCH, 3, 2, FBLK, NX * YZ)
            density = triad_density(donor_modes, slopes, receiver)
            density = jnp.where(offset < live_count, density, jnp.zeros_like(density))
            return (running + density, lax.optimization_barrier(jnp.sum(density, axis=1)))
        summed, columns = lax.scan(one_offset, jnp.zeros((FBLK, NX * YZ), jnp.float32), jnp.arange(FBLK, dtype=jnp.int32))
        current = lax.dynamic_slice_in_dim(transfer, start_k, FBLK, 0)
        transfer = lax.dynamic_update_slice_in_dim(transfer, current + summed * scale_field, start_k, 0)
        totals_list.append(columns.T * scale_triad)
    return (transfer.reshape(KF, NX, YZ), jnp.stack(totals_list))
```

```python
import math

import jax
import jax.numpy as jnp
from jax import lax
from jax.experimental import pallas as pl
from jax.experimental.pallas import tpu as pltpu
from jax.sharding import PartitionSpec as P

FBLK = 64
CZ = 16
AUNROLL = 8


def triad_kernel(list_ref, count_ref, modes_ref, halo_ref, field_ref, triad_ref, donors, receivers):
    field_ref[...] = jnp.zeros_like(field_ref)
    triad_ref[...] = jnp.zeros_like(triad_ref)
    rows, lanes = modes_ref.shape[2:]
    lane = lax.broadcasted_iota(jnp.int32, (rows, lanes), 1)
    plane = lax.broadcasted_iota(jnp.int32, (rows, lanes), 0) % 4

    for listed in range(2):
        start_k = list_ref[listed, 0] * FBLK
        start_l = list_ref[listed, 1] * FBLK
        start_m = start_k + start_l

        def prepare_donor(a, _):
            for i in range(3):
                real = modes_ref[2 * i, start_k + a].astype(jnp.float32)
                imag = modes_ref[2 * i + 1, start_k + a].astype(jnp.float32)
                donors[a, i] = real
                donors[a, 3 + i] = real + imag
                donors[a, 6 + i] = imag - real
            return 0

        def prepare_receiver(m, _):
            for i in range(3):
                real = modes_ref[2 * i, start_m + m].astype(jnp.float32)
                imag = modes_ref[2 * i + 1, start_m + m].astype(jnp.float32)
                receivers[m, i] = real + imag
                receivers[m, 3 + i] = real
                receivers[m, 6 + i] = imag
            return 0

        lax.fori_loop(0, FBLK, prepare_donor, 0)
        lax.fori_loop(0, 2 * FBLK, prepare_receiver, 0)

        def gradient(component, c):
            u = modes_ref[component, start_l + c].astype(jnp.float32)
            edge = halo_ref[listed, component, c].astype(jnp.float32)
            first = jnp.where(plane == 3, edge, pltpu.roll(u, rows - 1, 0)) - jnp.where(
                plane == 0, edge, pltpu.roll(u, 1, 0)
            )
            second = jnp.where(lane < lanes - CZ, pltpu.roll(u, lanes - CZ, 1), 0.0) - jnp.where(
                lane >= CZ, pltpu.roll(u, CZ, 1), 0.0
            )
            third = jnp.where(lane % CZ != CZ - 1, pltpu.roll(u, lanes - 1, 1), 0.0) - jnp.where(
                lane % CZ != 0, pltpu.roll(u, 1, 1), 0.0
            )
            return (first * -0.5, second * -0.5, third * -0.5)

        def one_offset(c, _):
            forms = []
            for i in range(3):
                real = gradient(2 * i, c)
                imag = gradient(2 * i + 1, c)
                forms.append(
                    [
                        [real[j] + imag[j] for j in range(3)],
                        [-imag[j] for j in range(3)],
                        [real[j] for j in range(3)],
                    ]
                )

            def some_donors(step, sums):
                for offset in range(AUNROLL):
                    a = step * AUNROLL + offset
                    total = None
                    for r in range(3):
                        given = [donors[a, 3 * r + j] for j in range(3)]
                        for i in range(3):
                            g = forms[i][r]
                            term = (given[0] * g[0] + given[1] * g[1] + given[2] * g[2]) * receivers[
                                a + c, 3 * r + i
                            ]
                            total = term if total is None else total + term
                    field_ref[start_k + a] += total
                    row = jnp.sum(total, axis=1, keepdims=True)
                    sums = jnp.where(lane == a, row, sums)
                return sums

            sums = lax.fori_loop(0, FBLK // AUNROLL, some_donors, jnp.zeros((rows, lanes), jnp.float32))
            triad_ref[listed, c] = sums
            return 0

        lax.fori_loop(0, count_ref[listed], one_offset, 0)


def per_device(velocity_modes, block_list, counts):
    blocks_here, _, _, freq_count, planes, cross_cells = velocity_modes.shape
    donors_span = (freq_count // FBLK - 1) * FBLK
    welch_all = blocks_here * lax.axis_size("blk")
    cells_all = planes * lax.axis_size("cell") * cross_cells
    scale_field = 0.25 / math.sqrt(welch_all * FBLK)
    scale_triad = 0.25 / math.sqrt(welch_all * cells_all)
    rows = blocks_here * planes

    needed = jnp.stack(
        [
            lax.dynamic_slice_in_dim(velocity_modes[:, :, :, :, :: planes - 1], block_list[n, 1] * FBLK, FBLK, 3)
            for n in range(2)
        ]
    )
    count = lax.axis_size("cell")
    below = lax.ppermute(needed[:, :, :, :, :, 1], "cell", [(i, i + 1) for i in range(count - 1)])
    above = lax.ppermute(needed[:, :, :, :, :, 0], "cell", [(i + 1, i) for i in range(count - 1)])
    empty = jnp.zeros_like(below)
    halo = jnp.stack([below, empty, empty, above], axis=5)
    halo = halo.transpose(0, 2, 3, 4, 1, 5, 6).reshape(2, 6, FBLK, rows, cross_cells)
    modes = velocity_modes.transpose(1, 2, 3, 0, 4, 5).reshape(6, freq_count, rows, cross_cells)

    vmem = pl.BlockSpec(memory_space=pltpu.VMEM)
    smem = pl.BlockSpec(memory_space=pltpu.SMEM)
    field, triads = pl.pallas_call(
        triad_kernel,
        out_shape=(
            jax.ShapeDtypeStruct((donors_span, rows, cross_cells), jnp.float32),
            jax.ShapeDtypeStruct((2, FBLK, rows, cross_cells), jnp.float32),
        ),
        in_specs=[smem, smem, vmem, vmem],
        out_specs=(vmem, vmem),
        scratch_shapes=[
            pltpu.VMEM((FBLK, 9, rows, cross_cells), jnp.float32),
            pltpu.VMEM((2 * FBLK, 9, rows, cross_cells), jnp.float32),
        ],
        compiler_params=pltpu.CompilerParams(vmem_limit_bytes=56 << 20),
    )(block_list, counts, modes, halo)

    triads_local = jnp.sum(triads, axis=2)[:, :, :FBLK].transpose(0, 2, 1) * scale_triad
    triad_sums = lax.psum(triads_local, ("cell", "blk"))
    local_field = field.reshape(donors_span, blocks_here, planes, cross_cells).sum(1) * scale_field
    field_share = lax.psum_scatter(local_field, "blk", scatter_dimension=0, tiled=True)
    return (field_share, triad_sums)


def solution(mesh):
    return jax.shard_map(
        per_device,
        mesh=mesh,
        in_specs=(P("blk", None, None, None, "cell", None), P(), P()),
        out_specs=(P("blk", "cell", None), P()),
        check_vma=False,
    )
```

```python
import functools
import math

import jax
import jax.numpy as jnp
from jax import lax
from jax.experimental import pallas as pl
from jax.experimental.pallas import tpu as pltpu
from jax.sharding import PartitionSpec as P

FBLK = 64
CZ = 16
AUNROLL = 8
NEAR = 16


def triad_kernel(list_ref, count_ref, modes_ref, halo_ref, field_ref, triad_ref, donors, receivers):
    field_ref[...] = jnp.zeros_like(field_ref)
    triad_ref[...] = jnp.zeros_like(triad_ref)
    rows, lanes = modes_ref.shape[2:]
    lane = lax.broadcasted_iota(jnp.int32, (rows, lanes), 1)
    plane = lax.broadcasted_iota(jnp.int32, (rows, lanes), 0) % 4

    for listed in range(2):
        start_k = list_ref[listed, 0] * FBLK
        start_l = list_ref[listed, 1] * FBLK
        start_m = start_k + start_l

        def prepare_donor(a, _):
            for i in range(3):
                real = modes_ref[2 * i, start_k + a].astype(jnp.float32)
                imag = modes_ref[2 * i + 1, start_k + a].astype(jnp.float32)
                donors[a, i] = real
                donors[a, 3 + i] = real + imag
                donors[a, 6 + i] = imag - real
            return 0

        def prepare_receiver(m, _):
            for i in range(3):
                real = modes_ref[2 * i, start_m + m].astype(jnp.float32)
                imag = modes_ref[2 * i + 1, start_m + m].astype(jnp.float32)
                receivers[m, i] = real + imag
                receivers[m, 3 + i] = real
                receivers[m, 6 + i] = imag
            return 0

        lax.fori_loop(0, FBLK, prepare_donor, 0)
        lax.fori_loop(0, 2 * FBLK, prepare_receiver, 0)

        def gradient(component, c):
            u = modes_ref[component, start_l + c].astype(jnp.float32)
            edge = halo_ref[listed, component, c].astype(jnp.float32)
            first = jnp.where(plane == 3, edge, pltpu.roll(u, rows - 1, 0)) - jnp.where(
                plane == 0, edge, pltpu.roll(u, 1, 0)
            )
            second = jnp.where(lane < lanes - CZ, pltpu.roll(u, lanes - CZ, 1), 0.0) - jnp.where(
                lane >= CZ, pltpu.roll(u, CZ, 1), 0.0
            )
            third = jnp.where(lane % CZ != CZ - 1, pltpu.roll(u, lanes - 1, 1), 0.0) - jnp.where(
                lane % CZ != 0, pltpu.roll(u, 1, 1), 0.0
            )
            return (first * -0.5, second * -0.5, third * -0.5)

        def one_offset(c, _):
            forms = []
            for i in range(3):
                real = gradient(2 * i, c)
                imag = gradient(2 * i + 1, c)
                forms.append(
                    [
                        [real[j] + imag[j] for j in range(3)],
                        [-imag[j] for j in range(3)],
                        [real[j] for j in range(3)],
                    ]
                )

            def some_donors(step, sums):
                for offset in range(AUNROLL):
                    a = step * AUNROLL + offset
                    total = None
                    for r in range(3):
                        given = [donors[a, 3 * r + j] for j in range(3)]
                        for i in range(3):
                            g = forms[i][r]
                            term = (given[0] * g[0] + given[1] * g[1] + given[2] * g[2]) * receivers[
                                a + c, 3 * r + i
                            ]
                            total = term if total is None else total + term
                    field_ref[start_k + a] += total
                    row = jnp.sum(total, axis=1, keepdims=True)
                    sums = jnp.where(lane == a, row, sums)
                return sums

            sums = lax.fori_loop(0, FBLK // AUNROLL, some_donors, jnp.zeros((rows, lanes), jnp.float32))
            triad_ref[listed, c] = sums
            return 0

        lax.fori_loop(0, count_ref[listed], one_offset, 0)


def exchange_kernel(
    scale_field,
    scale_triad,
    field_ref,
    sums_ref,
    share_ref,
    triad_ref,
    field_in,
    blk_in,
    x_in,
    zc_in,
    whole,
    sent,
    field_got,
    blk_got,
    x_got,
    zc_got,
    whole_got,
):
    cell = lax.axis_index("cell")
    blk = lax.axis_index("blk")
    blks = field_ref.shape[0]
    part = sums_ref.shape[0] // blks
    near = zc_in.shape[0]
    far = x_in.shape[0]
    x_at = cell // near
    zc_at = lax.rem(cell, near)
    mesh_id = pl.DeviceIdType.MESH

    def blk_peer(step):
        return (cell, lax.rem(blk + step, blks))

    def x_peer(step):
        return (lax.rem(x_at + step, far) * near + zc_at, blk)

    def zc_peer(step):
        return (x_at * near + lax.rem(zc_at + step, near), blk)

    barrier = pltpu.get_barrier_semaphore()
    peers = [blk_peer(s) for s in range(1, blks)]
    peers += [x_peer(s) for s in range(1, far)]
    peers += [zc_peer(s) for s in range(1, near)]
    for peer in peers:
        pl.semaphore_signal(barrier, inc=1, device_id=peer, device_id_type=mesh_id)
    pl.semaphore_wait(barrier, len(peers))

    copies = []

    def send(source, target, got, peer):
        copy = pltpu.make_async_remote_copy(
            src_ref=source,
            dst_ref=target,
            send_sem=sent.at[len(copies)],
            recv_sem=got,
            device_id=peer,
            device_id_type=mesh_id,
        )
        copy.start()
        copies.append(copy)
        return copy

    own_rows = pl.ds(pl.multiple_of(blk * part, part), part)
    first = []
    for s in range(1, blks):
        rows = pl.ds(pl.multiple_of(lax.rem(blk + s, blks) * part, part), part)
        first.append(send(sums_ref.at[rows], blk_in.at[s - 1], blk_got.at[s - 1], blk_peer(s)))
    fields = []
    for s in range(1, blks):
        fields.append(
            send(field_ref.at[lax.rem(blk + s, blks)], field_in.at[s - 1], field_got.at[s - 1], blk_peer(s))
        )
    for copy in first:
        copy.wait_recv()
    total = sums_ref[own_rows, :]
    for s in range(1, blks):
        total = total + blk_in[s - 1]
    x_in[x_at] = total
    second = [send(x_in.at[x_at], x_in.at[x_at], x_got.at[s - 1], x_peer(s)) for s in range(1, far)]
    for copy in second:
        copy.wait_recv()
    total = x_in[0]
    for k in range(1, far):
        total = total + x_in[k]
    zc_in[zc_at] = total
    third = [send(zc_in.at[zc_at], zc_in.at[zc_at], zc_got.at[s - 1], zc_peer(s)) for s in range(1, near)]
    for copy in third:
        copy.wait_recv()
    total = zc_in[0]
    for k in range(1, near):
        total = total + zc_in[k]
    whole[own_rows, :] = total
    fourth = [send(whole.at[own_rows], whole.at[own_rows], whole_got.at[s - 1], blk_peer(s)) for s in range(1, blks)]
    for copy in fields:
        copy.wait_recv()
    share = field_ref[blk]
    for s in range(1, blks):
        share = share + field_in[s - 1]
    share_ref[...] = share * scale_field
    for copy in fourth:
        copy.wait_recv()
    width = triad_ref.shape[2]
    for n in range(triad_ref.shape[0]):
        triad_ref[n] = whole[:, n * width : (n + 1) * width] * scale_triad
    for copy in copies:
        copy.wait_send()


def exchange(local_field, sums, scale_field, scale_triad):
    blks = lax.axis_size("blk")
    near = NEAR
    far = lax.axis_size("cell") // near
    share = local_field.shape[0] // blks
    chunks = local_field.reshape(blks, share, *local_field.shape[1:])
    part = sums.shape[0] // blks
    vmem = pl.BlockSpec(memory_space=pltpu.VMEM)
    dma = pltpu.SemaphoreType.DMA
    sends = 3 * (blks - 1) + (far - 1) + (near - 1)
    return pl.pallas_call(
        functools.partial(exchange_kernel, scale_field, scale_triad),
        out_shape=(
            jax.ShapeDtypeStruct(chunks.shape[1:], jnp.float32),
            jax.ShapeDtypeStruct((2, FBLK, FBLK), jnp.float32),
        ),
        in_specs=[vmem, vmem],
        out_specs=(vmem, vmem),
        scratch_shapes=[
            pltpu.VMEM((blks - 1,) + chunks.shape[1:], jnp.float32),
            pltpu.VMEM((blks - 1, part, sums.shape[1]), jnp.float32),
            pltpu.VMEM((far, part, sums.shape[1]), jnp.float32),
            pltpu.VMEM((near, part, sums.shape[1]), jnp.float32),
            pltpu.VMEM(sums.shape, jnp.float32),
            dma((sends,)),
            dma((blks - 1,)),
            dma((blks - 1,)),
            dma((far - 1,)),
            dma((near - 1,)),
            dma((blks - 1,)),
        ],
        compiler_params=pltpu.CompilerParams(collective_id=0, has_side_effects=True),
    )(chunks, sums)


def per_device(velocity_modes, block_list, counts):
    blocks_here, _, _, freq_count, planes, cross_cells = velocity_modes.shape
    donors_span = (freq_count // FBLK - 1) * FBLK
    welch_all = blocks_here * lax.axis_size("blk")
    cells_all = planes * lax.axis_size("cell") * cross_cells
    scale_field = 0.25 / math.sqrt(welch_all * FBLK)
    scale_triad = 0.25 / math.sqrt(welch_all * cells_all)
    rows = blocks_here * planes

    needed = [lax.dynamic_slice_in_dim(velocity_modes, block_list[n, 1] * FBLK, FBLK, 3) for n in range(2)]
    low_planes = jnp.stack([part[:, :, :, :, 0] for part in needed])
    high_planes = jnp.stack([part[:, :, :, :, planes - 1] for part in needed])
    count = lax.axis_size("cell")
    below = lax.ppermute(high_planes, "cell", [(i, i + 1) for i in range(count - 1)])
    above = lax.ppermute(low_planes, "cell", [(i + 1, i) for i in range(count - 1)])
    empty = jnp.zeros_like(below)
    halo = jnp.stack([below, empty, empty, above], axis=5)
    halo = halo.transpose(0, 2, 3, 4, 1, 5, 6).reshape(2, 6, FBLK, rows, cross_cells)
    modes = velocity_modes.transpose(1, 2, 3, 0, 4, 5).reshape(6, freq_count, rows, cross_cells)

    vmem = pl.BlockSpec(memory_space=pltpu.VMEM)
    smem = pl.BlockSpec(memory_space=pltpu.SMEM)
    field, triads = pl.pallas_call(
        triad_kernel,
        out_shape=(
            jax.ShapeDtypeStruct((donors_span, rows, cross_cells), jnp.float32),
            jax.ShapeDtypeStruct((2, FBLK, rows, cross_cells), jnp.float32),
        ),
        in_specs=[smem, smem, vmem, vmem],
        out_specs=(vmem, vmem),
        scratch_shapes=[
            pltpu.VMEM((FBLK, 9, rows, cross_cells), jnp.float32),
            pltpu.VMEM((2 * FBLK, 9, rows, cross_cells), jnp.float32),
        ],
        compiler_params=pltpu.CompilerParams(vmem_limit_bytes=56 << 20),
    )(block_list, counts, modes, halo)

    lists = triads.shape[0]
    sums = jnp.sum(triads, axis=2)[:, :, :FBLK].transpose(2, 0, 1).reshape(FBLK, lists * FBLK)
    local_field = field.reshape(donors_span, blocks_here, planes, cross_cells).sum(1)
    return exchange(local_field, sums, scale_field, scale_triad)


def solution(mesh):
    return jax.shard_map(
        per_device,
        mesh=mesh,
        in_specs=(P("blk", None, None, None, "cell", None), P(), P()),
        out_specs=(P("blk", "cell", None), P()),
        check_vma=False,
    )
```

```python
import functools
import math

import jax
import jax.numpy as jnp
from jax import lax
from jax.experimental import pallas as pl
from jax.experimental.pallas import tpu as pltpu
from jax.sharding import PartitionSpec as P

FBLK = 64
CZ = 16
VARIANTS = (2, 4)
NEAR = 16


def slot_transpose(parts):
    lane = lax.broadcasted_iota(jnp.int32, parts[0].shape, 1)
    width = parts[0].shape[1]
    parts = list(parts)
    for k in (1, 2, 4):
        keep = (lane // CZ) & k == 0
        for v in range(8):
            if v & k == 0:
                a, b = parts[v], parts[v | k]
                parts[v] = jnp.where(keep, a, pltpu.roll(b, CZ * k, 1))
                parts[v | k] = jnp.where(keep, pltpu.roll(a, width - CZ * k, 1), b)
    return parts


def triad_kernel(
    list_ref,
    count_ref,
    modes_ref,
    below_ref,
    above_ref,
    field_ref,
    sums_ref,
    grouped,
    left_a,
    left_b,
    right_a,
    right_b,
    window_a,
    window_b,
    pair_sums,
    rows_out,
    triads,
):
    lefts, rights, windows = (left_a, left_b), (right_a, right_b), (window_a, window_b)
    lanes = modes_ref.shape[4]
    field_ref[...] = jnp.zeros_like(field_ref)
    right_a[...] = jnp.zeros_like(right_a)
    right_b[...] = jnp.zeros_like(right_b)

    def regroup(index, _):
        comp = index % 6
        b = index // 6
        for p in range(4):
            for block in range(4):
                rows = modes_ref[b, comp, p, block * FBLK : (block + 1) * FBLK, :].astype(jnp.float32)
                parts = slot_transpose([rows[8 * v : 8 * v + 8] for v in range(8)])
                for y in range(8):
                    grouped[b, 8 * p + y, comp, block] = parts[y]
        return 0

    lax.fori_loop(0, 12, regroup, 0)

    lane = lax.broadcasted_iota(jnp.int32, (16, lanes), 1)
    row = lax.broadcasted_iota(jnp.int32, (16, lanes), 0)
    z = lane % CZ
    slot8 = lax.broadcasted_iota(jnp.int32, (8, lanes), 1) // CZ
    row8 = lax.broadcasted_iota(jnp.int32, (8, lanes), 0)
    picked = (slot8 == row8).astype(jnp.float32)
    zero = jnp.zeros((16, lanes), jnp.bfloat16)

    def fill_left(plane, index, left):
        n = plane // 4
        p = plane % 4
        at_l = list_ref[n, 1]
        i = index % 3
        b = index // 3
        for cc in range(4):
            first = pl.multiple_of(at_l * FBLK + cc * 16, 16)
            own = pl.ds(cc * 16, 16)
            shifted = []
            for part in range(2):
                comp = 2 * i + part
                u = modes_ref[b, comp, p, pl.ds(first, 16), :]
                up = modes_ref[b, comp, jnp.minimum(p + 1, 3), pl.ds(first, 16), :]
                down = modes_ref[b, comp, jnp.maximum(p - 1, 0), pl.ds(first, 16), :]
                up = jnp.where(p == 3, above_ref[n, b, comp, own, :], up)
                down = jnp.where(p == 0, below_ref[n, b, comp, own, :], down)
                shifted.append(
                    slot_transpose(
                        [
                            up,
                            -down,
                            jnp.where(lane < lanes - CZ, pltpu.roll(u, lanes - CZ, 1), zero),
                            jnp.where(lane >= CZ, -pltpu.roll(u, CZ, 1), zero),
                            jnp.where(z < CZ - 1, pltpu.roll(u, lanes - 1, 1), zero),
                            jnp.where(z > 0, -pltpu.roll(u, 1, 1), zero),
                            zero,
                            zero,
                        ]
                    )
                )
            at = pl.multiple_of((cc * 3 + i) * 32, 32)
            for y in range(8):
                real = shifted[0][y]
                imag = shifted[1][y]
                left[b, y, pl.ds(at, 16), :lanes] = real
                left[b, y, pl.ds(at, 16), lanes:] = -imag
                left[b, y, pl.ds(at + 16, 16), :lanes] = imag
                left[b, y, pl.ds(at + 16, 16), lanes:] = real

    def build(step, right, window):
        n = step // 32
        group = step % 32
        at_k = list_ref[n, 0]
        at_m = at_k + list_ref[n, 1]
        for b in range(2):
            for comp in range(6):
                now = grouped[b, group, comp, at_m]
                later = grouped[b, group, comp, at_m + 1]
                window[b, comp, 0:8, :] = now
                for g in range(1, 8):
                    window[b, comp, 8 * g : 8 * g + 8, :] = jnp.where(
                        slot8 < 8 - g,
                        pltpu.roll(now, lanes - CZ * g, 1),
                        pltpu.roll(later, lanes - CZ * g, 1),
                    )
                window[b, comp, 64:72, :] = later
                j, part = comp // 2, comp % 2
                for a in range(8):
                    donor = grouped[b, group, comp, at_k, pl.ds(a, 16, stride=0), :]
                    spread = jnp.where(z == row, donor, 0.0).astype(jnp.bfloat16)
                    for side in range(2):
                        top = part * lanes + (2 * j + side) * 16
                        right[b, top : top + 16, a * lanes : (a + 1) * lanes] = spread

    def contract(y, chunks, live, left, right, window):
        for a2 in range(4):
            products = [
                jnp.dot(
                    left[b, y, : chunks * 96, :],
                    right[b, :, a2 * 2 * lanes : (a2 + 1) * 2 * lanes],
                    preferred_element_type=jnp.float32,
                )
                for b in range(2)
            ]
            for half in range(2):
                a = 2 * a2 + half
                kept = None
                for ch in range(2 * chunks):
                    total = None
                    for b in range(2):
                        for comp in range(6):
                            at = (ch // 2 * 6 + comp) * 16 + 8 * (ch % 2)
                            term = (
                                products[b][at : at + 8, half * lanes : (half + 1) * lanes]
                                * window[b, comp, 8 * ch + a : 8 * ch + a + 8, :]
                            )
                            total = term if total is None else total + term
                    pair_sums[a, 8 * ch : 8 * ch + 8, :] += total
                    masked = jnp.where(row8 < live - 8 * ch, total, 0.0)
                    kept = masked if kept is None else kept + masked
                rows_out[y, a : a + 1, :] = jnp.sum(kept, axis=0, keepdims=True)

    lax.fori_loop(0, 6, lambda index, _: (fill_left(0, index, left_a), 0)[1], 0)
    build(0, right_a, window_a)

    def plane_pair(t, _):
        n = t // 2
        at_k = list_ref[n, 0]
        live = count_ref[n]

        @pl.when(t % 2 == 0)
        def _():
            pair_sums[...] = jnp.zeros_like(pair_sums)

        for parity in range(2):
            plane = 2 * t + parity

            def group_pair(y2, _):
                for half in range(2):
                    y = 2 * y2 + half
                    below = 0
                    for chunks in VARIANTS:

                        @pl.when((live > 16 * below) & (live <= 16 * chunks))
                        def _():
                            contract(y, chunks, live, lefts[parity], rights[half], windows[half])
                            build(jnp.minimum(plane * 8 + y + 1, 63), rights[1 - half], windows[1 - half])
                            fill_left(jnp.minimum(plane + 1, 7), jnp.minimum(y, 5), lefts[1 - parity])

                        below = chunks
                return 0

            lax.fori_loop(0, 4, group_pair, 0)
            parts = slot_transpose([rows_out[y] for y in range(8)])
            for v in range(8):
                field_ref[at_k * 8 + v, plane % 4] += parts[v]

        @pl.when(t % 2 == 1)
        def _():
            for a in range(8):
                triads[n, pl.ds(a, 8, stride=8), :] = lax.dot_general(
                    picked,
                    pair_sums[a],
                    (((1,), (1,)), ((), ())),
                    precision=lax.Precision.HIGHEST,
                    preferred_element_type=jnp.float32,
                )

        return 0

    lax.fori_loop(0, 4, plane_pair, 0)
    column = lax.broadcasted_iota(jnp.int32, (FBLK, FBLK), 1)
    for n in range(2):
        sums_ref[:, n * FBLK : (n + 1) * FBLK] = jnp.where(column < count_ref[n], triads[n], 0.0)


def run_triads(block_list, counts, modes, below, above):
    planes, freq_count, cross_cells = modes.shape[2:]
    donors_span = (freq_count // FBLK - 1) * FBLK
    vmem = pl.BlockSpec(memory_space=pltpu.VMEM)
    smem = pl.BlockSpec(memory_space=pltpu.SMEM)
    return pl.pallas_call(
        triad_kernel,
        out_shape=(
            jax.ShapeDtypeStruct((donors_span // 8, planes, 8, cross_cells), jnp.float32),
            jax.ShapeDtypeStruct((FBLK, 2 * FBLK), jnp.float32),
        ),
        in_specs=[smem, smem, vmem, vmem, vmem],
        out_specs=(vmem, vmem),
        scratch_shapes=[
            pltpu.VMEM((2, 32, 6, 4, 8, cross_cells), jnp.float32),
            pltpu.VMEM((2, 8, 384, 2 * cross_cells), jnp.bfloat16),
            pltpu.VMEM((2, 8, 384, 2 * cross_cells), jnp.bfloat16),
            pltpu.VMEM((2, 2 * cross_cells, 8 * cross_cells), jnp.bfloat16),
            pltpu.VMEM((2, 2 * cross_cells, 8 * cross_cells), jnp.bfloat16),
            pltpu.VMEM((2, 6, 72, cross_cells), jnp.float32),
            pltpu.VMEM((2, 6, 72, cross_cells), jnp.float32),
            pltpu.VMEM((8, FBLK, cross_cells), jnp.float32),
            pltpu.VMEM((8, 8, cross_cells), jnp.float32),
            pltpu.VMEM((2, FBLK, FBLK), jnp.float32),
        ],
        compiler_params=pltpu.CompilerParams(vmem_limit_bytes=40 << 20),
    )(block_list, counts, modes, below, above)


def exchange_kernel(
    scale_field,
    scale_triad,
    field_ref,
    sums_ref,
    share_ref,
    triad_ref,
    field_in,
    blk_in,
    x_in,
    zc_in,
    whole,
    sent,
    field_got,
    blk_got,
    x_got,
    zc_got,
    whole_got,
):
    cell = lax.axis_index("cell")
    blk = lax.axis_index("blk")
    blks = field_ref.shape[0]
    part = sums_ref.shape[0] // blks
    near = zc_in.shape[0]
    far = x_in.shape[0]
    x_at = cell // near
    zc_at = lax.rem(cell, near)
    mesh_id = pl.DeviceIdType.MESH

    def blk_peer(step):
        return (cell, lax.rem(blk + step, blks))

    def x_peer(step):
        return (lax.rem(x_at + step, far) * near + zc_at, blk)

    def zc_peer(step):
        return (x_at * near + lax.rem(zc_at + step, near), blk)

    barrier = pltpu.get_barrier_semaphore()
    peers = [blk_peer(s) for s in range(1, blks)]
    peers += [x_peer(s) for s in range(1, far)]
    peers += [zc_peer(s) for s in range(1, near)]
    for peer in peers:
        pl.semaphore_signal(barrier, inc=1, device_id=peer, device_id_type=mesh_id)
    pl.semaphore_wait(barrier, len(peers))

    copies = []

    def send(source, target, got, peer):
        copy = pltpu.make_async_remote_copy(
            src_ref=source,
            dst_ref=target,
            send_sem=sent.at[len(copies)],
            recv_sem=got,
            device_id=peer,
            device_id_type=mesh_id,
        )
        copy.start()
        copies.append(copy)
        return copy

    own_rows = pl.ds(pl.multiple_of(blk * part, part), part)
    first = []
    for s in range(1, blks):
        rows = pl.ds(pl.multiple_of(lax.rem(blk + s, blks) * part, part), part)
        first.append(send(sums_ref.at[rows], blk_in.at[s - 1], blk_got.at[s - 1], blk_peer(s)))
    fields = []
    for s in range(1, blks):
        fields.append(
            send(field_ref.at[lax.rem(blk + s, blks)], field_in.at[s - 1], field_got.at[s - 1], blk_peer(s))
        )
    for copy in first:
        copy.wait_recv()
    total = sums_ref[own_rows, :]
    for s in range(1, blks):
        total = total + blk_in[s - 1]
    x_in[x_at] = total
    second = [send(x_in.at[x_at], x_in.at[x_at], x_got.at[s - 1], x_peer(s)) for s in range(1, far)]
    for copy in second:
        copy.wait_recv()
    total = x_in[0]
    for k in range(1, far):
        total = total + x_in[k]
    zc_in[zc_at] = total
    third = [send(zc_in.at[zc_at], zc_in.at[zc_at], zc_got.at[s - 1], zc_peer(s)) for s in range(1, near)]
    for copy in third:
        copy.wait_recv()
    total = zc_in[0]
    for k in range(1, near):
        total = total + zc_in[k]
    whole[own_rows, :] = total
    fourth = [send(whole.at[own_rows], whole.at[own_rows], whole_got.at[s - 1], blk_peer(s)) for s in range(1, blks)]
    for copy in fields:
        copy.wait_recv()
    share = field_ref[blk]
    for s in range(1, blks):
        share = share + field_in[s - 1]
    share_ref[...] = share * scale_field
    for copy in fourth:
        copy.wait_recv()
    width = triad_ref.shape[2]
    for n in range(triad_ref.shape[0]):
        triad_ref[n] = whole[:, n * width : (n + 1) * width] * scale_triad
    for copy in copies:
        copy.wait_send()


def exchange(local_field, sums, scale_field, scale_triad):
    blks = lax.axis_size("blk")
    near = NEAR
    far = lax.axis_size("cell") // near
    share = local_field.shape[0] // blks
    chunks = local_field.reshape(blks, share, *local_field.shape[1:])
    part = sums.shape[0] // blks
    vmem = pl.BlockSpec(memory_space=pltpu.VMEM)
    dma = pltpu.SemaphoreType.DMA
    sends = 3 * (blks - 1) + (far - 1) + (near - 1)
    return pl.pallas_call(
        functools.partial(exchange_kernel, scale_field, scale_triad),
        out_shape=(
            jax.ShapeDtypeStruct(chunks.shape[1:], jnp.float32),
            jax.ShapeDtypeStruct((2, FBLK, FBLK), jnp.float32),
        ),
        in_specs=[vmem, vmem],
        out_specs=(vmem, vmem),
        scratch_shapes=[
            pltpu.VMEM((blks - 1,) + chunks.shape[1:], jnp.float32),
            pltpu.VMEM((blks - 1, part, sums.shape[1]), jnp.float32),
            pltpu.VMEM((far, part, sums.shape[1]), jnp.float32),
            pltpu.VMEM((near, part, sums.shape[1]), jnp.float32),
            pltpu.VMEM(sums.shape, jnp.float32),
            dma((sends,)),
            dma((blks - 1,)),
            dma((blks - 1,)),
            dma((far - 1,)),
            dma((near - 1,)),
            dma((blks - 1,)),
        ],
        compiler_params=pltpu.CompilerParams(collective_id=0, has_side_effects=True),
    )(chunks, sums)


def per_device(velocity_modes, block_list, counts):
    blocks_here, _, _, freq_count, planes, cross_cells = velocity_modes.shape
    welch_all = blocks_here * lax.axis_size("blk")
    cells_all = planes * lax.axis_size("cell") * cross_cells
    scale_field = -0.5 * 0.25 / math.sqrt(welch_all * FBLK)
    scale_triad = -0.5 * 0.25 / math.sqrt(welch_all * cells_all)

    modes = velocity_modes.reshape(blocks_here, 6, freq_count, planes, cross_cells).swapaxes(2, 3)
    low_planes, high_planes = (
        jnp.stack(
            [lax.dynamic_slice_in_dim(modes[:, :, p], block_list[n, 1] * FBLK, FBLK, 2) for n in range(2)]
        )
        for p in (0, planes - 1)
    )
    count = lax.axis_size("cell")
    below = lax.ppermute(high_planes, "cell", [(i, i + 1) for i in range(count - 1)])
    above = lax.ppermute(low_planes, "cell", [(i + 1, i) for i in range(count - 1)])

    field, sums = run_triads(block_list, counts, modes, below, above)
    share, triad_sums = exchange(field, sums, scale_field, scale_triad)
    return (share.swapaxes(1, 2).reshape(-1, planes, cross_cells), triad_sums)


def solution(mesh):
    return jax.shard_map(
        per_device,
        mesh=mesh,
        in_specs=(P("blk", None, None, None, "cell", None), P(), P()),
        out_specs=(P("blk", "cell", None), P()),
        check_vma=False,
    )
```

```python
import functools
import math

import jax
import jax.numpy as jnp
from jax import lax
from jax.experimental import pallas as pl
from jax.experimental.pallas import tpu as pltpu
from jax.sharding import PartitionSpec as P

FBLK = 64
CZ = 16
VARIANTS = (4,)
NEAR = 16


def slot_spread(parts):
    slot = lax.broadcasted_iota(jnp.int32, parts[0].shape, 1) // CZ
    for k in (1, 2, 4):
        odd = slot & k != 0
        parts = [jnp.where(odd, parts[(e + k) % 8], parts[e]) for e in range(8)]
    return [parts[-y % 8] for y in range(8)]


def slot_transpose(parts):
    width = parts[0].shape[1]
    turned = [parts[0]] + [pltpu.roll(parts[s], CZ * s, 1) for s in range(1, 8)]
    mixed = slot_spread(turned)
    return [mixed[0]] + [pltpu.roll(mixed[y], width - CZ * y, 1) for y in range(1, 8)]


def row_sums(parts):
    row = lax.broadcasted_iota(jnp.int32, parts[0].shape, 0)
    parts = list(parts)
    for k in (4, 2, 1):
        keep = row & k == 0
        merged = []
        for a in range(k):
            first, second = parts[a], parts[a + k]
            other = jnp.where(keep, second, first)
            if k == 4:
                other = pltpu.roll(other, 4, 0)
            else:
                other = jnp.where(keep, pltpu.roll(other, 8 - k, 0), pltpu.roll(other, k, 0))
            merged.append(jnp.where(keep, first, second) + other)
        parts = merged
    return parts[0]


def regroup_kernel(modes_ref, grouped, packed):
    def regroup(index, _):
        i = index % 3
        b = index // 3
        for p in range(4):
            for block in range(4):
                parts = []
                for v in range(8):
                    rows = pl.ds(block * FBLK + 8 * v, 8)
                    parts.append(
                        jnp.concatenate(
                            [modes_ref[b, 2 * i, p, rows, :], modes_ref[b, 2 * i + 1, p, rows, :]], axis=0
                        )
                    )
                parts = slot_transpose(parts)
                for y in range(8):
                    packed[b, 8 * p + y, i, block] = parts[y]
                    grouped[b, 8 * p + y, i, block] = parts[y].astype(jnp.float32)
        return 0

    lax.fori_loop(0, 6, regroup, 0)


def triad_kernel(
    list_ref,
    count_ref,
    modes_ref,
    below_ref,
    above_ref,
    grouped,
    packed,
    field_ref,
    sums_ref,
    left_a,
    left_b,
    right_a,
    right_b,
    window_a,
    window_b,
    pair_sums,
    rows_out,
    triads,
):
    lefts, rights, windows = (left_a, left_b), (right_a, right_b), (window_a, window_b)
    lanes = modes_ref.shape[4]
    field_ref[...] = jnp.zeros_like(field_ref)
    right_a[...] = jnp.zeros_like(right_a)
    right_b[...] = jnp.zeros_like(right_b)

    lane = lax.broadcasted_iota(jnp.int32, (16, lanes), 1)
    row = lax.broadcasted_iota(jnp.int32, (16, lanes), 0)
    z = lane % CZ
    slot = lane // CZ
    slot8 = lax.broadcasted_iota(jnp.int32, (8, lanes), 1) // CZ
    row8 = lax.broadcasted_iota(jnp.int32, (8, lanes), 0)
    picked = (slot8 == row8).astype(jnp.float32)
    zero = jnp.zeros((16, lanes), jnp.bfloat16)

    def fill_left(plane, index, left):
        n = plane // 4
        p = plane % 4
        at_l = list_ref[n, 1]
        i = index % 3
        b = index // 3
        for cc in range(4):
            first = pl.multiple_of(at_l * FBLK + cc * 16, 16)
            own = pl.ds(cc * 16, 16)
            shifted = []
            for part in range(2):
                comp = 2 * i + part
                u = modes_ref[b, comp, p, pl.ds(first, 16), :]
                up = modes_ref[b, comp, jnp.minimum(p + 1, 3), pl.ds(first, 16), :]
                down = modes_ref[b, comp, jnp.maximum(p - 1, 0), pl.ds(first, 16), :]
                up = jnp.where(p == 3, above_ref[n, b, comp, own, :], up)
                down = jnp.where(p == 0, below_ref[n, b, comp, own, :], down)
                shifted.append(
                    slot_spread(
                        [
                            up,
                            pltpu.roll(-down, CZ, 1),
                            jnp.where(slot == 1, zero, pltpu.roll(u, CZ, 1)),
                            jnp.where(slot == 3, zero, pltpu.roll(-u, 4 * CZ, 1)),
                            jnp.where(z == CZ - 1, zero, pltpu.roll(u, 4 * CZ - 1, 1)),
                            jnp.where(z == 0, zero, pltpu.roll(-u, 5 * CZ + 1, 1)),
                            zero,
                            zero,
                        ]
                    )
                )
            at = pl.multiple_of((cc * 3 + i) * 32, 32)
            for y in range(8):
                real = shifted[0][y]
                imag = shifted[1][y]
                left[b, y, pl.ds(at, 16), :lanes] = real
                left[b, y, pl.ds(at, 16), lanes:] = -imag
                left[b, y, pl.ds(at + 16, 16), :lanes] = imag
                left[b, y, pl.ds(at + 16, 16), lanes:] = real

    def build(step, right, window):
        n = step // 32
        group = step % 32
        at_k = list_ref[n, 0]
        at_m = at_k + list_ref[n, 1]
        y = group % 8
        for b in range(2):
            for i in range(3):
                now = packed[b, group, i, at_m]
                later = packed[b, group, i, at_m + 1]
                for g in range(9):
                    turned = now if g == 0 else later
                    if 0 < g < 8:
                        turned = pltpu.roll(jnp.where(slot >= g, now, later), lanes - CZ * g, 1)
                    turned = turned.astype(jnp.float32)
                    for part in range(2):
                        window[b, 2 * i + part, 8 * g : 8 * g + 8, :] = turned[8 * part : 8 * part + 8]
                for part in range(2):
                    for a in range(8):
                        donor = grouped[b, group, i, at_k, pl.ds(8 * part + a, 16, stride=0), :]
                        spread = jnp.where(z == row, donor, 0.0).astype(jnp.bfloat16)
                        for side in range(2):
                            top = pl.multiple_of(part * lanes + (y + 2 * i + side) % 8 * 16, 16)
                            right[b, pl.ds(top, 16), a * lanes : (a + 1) * lanes] = spread

    def contract(y, chunks, live, left, right, window):
        kept_all = []
        for a2 in range(4):
            products = [
                jnp.dot(
                    left[b, y, : chunks * 96, :],
                    right[b, :, a2 * 2 * lanes : (a2 + 1) * 2 * lanes],
                    preferred_element_type=jnp.float32,
                )
                for b in range(2)
            ]
            for half in range(2):
                a = 2 * a2 + half
                kept = None
                for ch in range(2 * chunks):
                    total = None
                    for b in range(2):
                        for comp in range(6):
                            at = (ch // 2 * 6 + comp) * 16 + 8 * (ch % 2)
                            term = (
                                products[b][at : at + 8, half * lanes : (half + 1) * lanes]
                                * window[b, comp, 8 * ch + a : 8 * ch + a + 8, :]
                            )
                            total = term if total is None else total + term
                    pair_sums[a, 8 * ch : 8 * ch + 8, :] += total
                    masked = jnp.where(row8 < live - 8 * ch, total, 0.0)
                    kept = masked if kept is None else kept + masked
                kept_all.append(kept)
        rows_out[y] = row_sums(kept_all)

    lax.fori_loop(0, 6, lambda index, _: (fill_left(0, index, left_a), 0)[1], 0)
    build(0, right_a, window_a)

    def plane_pair(t, _):
        n = t // 2
        at_k = list_ref[n, 0]
        live = count_ref[n]

        @pl.when(t % 2 == 0)
        def _():
            pair_sums[...] = jnp.zeros_like(pair_sums)

        for parity in range(2):
            plane = 2 * t + parity

            def group_pair(y2, _):
                for half in range(2):
                    y = 2 * y2 + half
                    below = 0
                    for chunks in VARIANTS:

                        @pl.when((live > 16 * below) & (live <= 16 * chunks))
                        def _():
                            contract(y, chunks, live, lefts[parity], rights[half], windows[half])
                            build(jnp.minimum(plane * 8 + y + 1, 63), rights[1 - half], windows[1 - half])
                            fill_left(jnp.minimum(plane + 1, 7), jnp.minimum(y, 5), lefts[1 - parity])

                        below = chunks
                return 0

            lax.fori_loop(0, 4, group_pair, 0)
            parts = slot_transpose([rows_out[y] for y in range(8)])
            for v in range(8):
                field_ref[at_k * 8 + v, plane % 4] += parts[v]

        @pl.when(t % 2 == 1)
        def _():
            for a in range(8):
                triads[n, pl.ds(a, 8, stride=8), :] = lax.dot_general(
                    picked,
                    pair_sums[a],
                    (((1,), (1,)), ((), ())),
                    precision=lax.Precision.HIGHEST,
                    preferred_element_type=jnp.float32,
                )

        return 0

    lax.fori_loop(0, 4, plane_pair, 0)
    column = lax.broadcasted_iota(jnp.int32, (FBLK, FBLK), 1)
    for n in range(2):
        sums_ref[:, n * FBLK : (n + 1) * FBLK] = jnp.where(column < count_ref[n], triads[n], 0.0)


def run_regroup(modes):
    lanes = modes.shape[4]
    vmem = pl.BlockSpec(memory_space=pltpu.VMEM)
    shape = (2, 32, 3, 4, 16, lanes)
    return pl.pallas_call(
        regroup_kernel,
        out_shape=(jax.ShapeDtypeStruct(shape, jnp.float32), jax.ShapeDtypeStruct(shape, jnp.bfloat16)),
        in_specs=[vmem],
        out_specs=(vmem, vmem),
        compiler_params=pltpu.CompilerParams(vmem_limit_bytes=16 << 20),
        cost_estimate=pl.CostEstimate(flops=40_000_000, bytes_accessed=13_000_000, transcendentals=0),
    )(modes)


def run_triads(block_list, counts, modes, below, above):
    grouped, packed = run_regroup(modes)
    planes, freq_count, cross_cells = modes.shape[2:]
    donors_span = (freq_count // FBLK - 1) * FBLK
    vmem = pl.BlockSpec(memory_space=pltpu.VMEM)
    smem = pl.BlockSpec(memory_space=pltpu.SMEM)
    return pl.pallas_call(
        triad_kernel,
        out_shape=(
            jax.ShapeDtypeStruct((donors_span // 8, planes, 8, cross_cells), jnp.float32),
            jax.ShapeDtypeStruct((FBLK, 2 * FBLK), jnp.float32),
        ),
        in_specs=[smem, smem, vmem, vmem, vmem, vmem, vmem],
        out_specs=(vmem, vmem),
        scratch_shapes=[
            pltpu.VMEM((2, 8, 384, 2 * cross_cells), jnp.bfloat16),
            pltpu.VMEM((2, 8, 384, 2 * cross_cells), jnp.bfloat16),
            pltpu.VMEM((2, 2 * cross_cells, 8 * cross_cells), jnp.bfloat16),
            pltpu.VMEM((2, 2 * cross_cells, 8 * cross_cells), jnp.bfloat16),
            pltpu.VMEM((2, 6, 72, cross_cells), jnp.float32),
            pltpu.VMEM((2, 6, 72, cross_cells), jnp.float32),
            pltpu.VMEM((8, FBLK, cross_cells), jnp.float32),
            pltpu.VMEM((8, 8, cross_cells), jnp.float32),
            pltpu.VMEM((2, FBLK, FBLK), jnp.float32),
        ],
        compiler_params=pltpu.CompilerParams(vmem_limit_bytes=32 << 20),
    )(block_list, counts, modes, below, above, grouped, packed)


def exchange_kernel(
    field_ref,
    sums_ref,
    share_ref,
    triad_ref,
    field_in,
    blk_in,
    x_in,
    zc_in,
    whole,
    sent,
    field_got,
    blk_got,
    x_got,
    zc_got,
    whole_got,
):
    cell = lax.axis_index("cell")
    blk = lax.axis_index("blk")
    blks = field_ref.shape[0]
    part = sums_ref.shape[0] // blks
    near = zc_in.shape[0]
    far = x_in.shape[0]
    x_at = cell // near
    zc_at = lax.rem(cell, near)
    mesh_id = pl.DeviceIdType.MESH

    def blk_peer(step):
        return (cell, lax.rem(blk + step, blks))

    def x_peer(step):
        return (lax.rem(x_at + step, far) * near + zc_at, blk)

    def zc_peer(step):
        return (x_at * near + lax.rem(zc_at + step, near), blk)

    barrier = pltpu.get_barrier_semaphore()
    peers = [blk_peer(s) for s in range(1, blks)]
    peers += [x_peer(s) for s in range(1, far)]
    peers += [zc_peer(s) for s in range(1, near)]
    for peer in peers:
        pl.semaphore_signal(barrier, inc=1, device_id=peer, device_id_type=mesh_id)
    pl.semaphore_wait(barrier, len(peers))

    copies = []

    def send(source, target, got, peer):
        copy = pltpu.make_async_remote_copy(
            src_ref=source,
            dst_ref=target,
            send_sem=sent.at[len(copies)],
            recv_sem=got,
            device_id=peer,
            device_id_type=mesh_id,
        )
        copy.start()
        copies.append(copy)
        return copy

    own_rows = pl.ds(pl.multiple_of(blk * part, part), part)
    first = []
    for s in range(1, blks):
        rows = pl.ds(pl.multiple_of(lax.rem(blk + s, blks) * part, part), part)
        first.append(send(sums_ref.at[rows], blk_in.at[s - 1], blk_got.at[s - 1], blk_peer(s)))
    fields = []
    for s in range(1, blks):
        fields.append(
            send(field_ref.at[lax.rem(blk + s, blks)], field_in.at[s - 1], field_got.at[s - 1], blk_peer(s))
        )
    for copy in first:
        copy.wait_recv()
    total = sums_ref[own_rows, :]
    for s in range(1, blks):
        total = total + blk_in[s - 1]
    x_in[x_at] = total
    second = [send(x_in.at[x_at], x_in.at[x_at], x_got.at[s - 1], x_peer(s)) for s in range(1, far)]
    for copy in second:
        copy.wait_recv()
    total = x_in[0]
    for k in range(1, far):
        total = total + x_in[k]
    zc_in[zc_at] = total
    third = [send(zc_in.at[zc_at], zc_in.at[zc_at], zc_got.at[s - 1], zc_peer(s)) for s in range(1, near)]
    for copy in third:
        copy.wait_recv()
    total = zc_in[0]
    for k in range(1, near):
        total = total + zc_in[k]
    whole[own_rows, :] = total
    fourth = [send(whole.at[own_rows], whole.at[own_rows], whole_got.at[s - 1], blk_peer(s)) for s in range(1, blks)]
    for copy in fields:
        copy.wait_recv()
    share = field_ref[blk]
    for s in range(1, blks):
        share = share + field_in[s - 1]
    share_ref[...] = share
    for copy in fourth:
        copy.wait_recv()
    triad_ref[...] = whole[...]
    for copy in copies:
        copy.wait_send()


def exchange(local_field, sums):
    blks = lax.axis_size("blk")
    near = NEAR
    far = lax.axis_size("cell") // near
    share = local_field.shape[0] // blks
    chunks = local_field.reshape(blks, share, *local_field.shape[1:])
    part = sums.shape[0] // blks
    vmem = pl.BlockSpec(memory_space=pltpu.VMEM)
    dma = pltpu.SemaphoreType.DMA
    sends = 3 * (blks - 1) + (far - 1) + (near - 1)
    return pl.pallas_call(
        exchange_kernel,
        out_shape=(
            jax.ShapeDtypeStruct(chunks.shape[1:], jnp.float32),
            jax.ShapeDtypeStruct(sums.shape, jnp.float32),
        ),
        in_specs=[vmem, vmem],
        out_specs=(vmem, vmem),
        scratch_shapes=[
            pltpu.VMEM((blks - 1,) + chunks.shape[1:], jnp.float32),
            pltpu.VMEM((blks - 1, part, sums.shape[1]), jnp.float32),
            pltpu.VMEM((far, part, sums.shape[1]), jnp.float32),
            pltpu.VMEM((near, part, sums.shape[1]), jnp.float32),
            pltpu.VMEM(sums.shape, jnp.float32),
            dma((sends,)),
            dma((blks - 1,)),
            dma((blks - 1,)),
            dma((far - 1,)),
            dma((near - 1,)),
            dma((blks - 1,)),
        ],
        compiler_params=pltpu.CompilerParams(collective_id=0, has_side_effects=True, vmem_limit_bytes=4 << 20),
    )(chunks, sums)


def finish_kernel(scale_field, scale_triad, share_ref, whole_ref, transfer_ref, triad_ref):
    groups, planes = share_ref.shape[:2]
    for g in range(groups):
        for p in range(planes):
            transfer_ref[8 * g : 8 * g + 8, p, :] = share_ref[g, p] * scale_field
    for n in range(2):
        triad_ref[n] = whole_ref[:, n * FBLK : (n + 1) * FBLK] * scale_triad


def finish(share, whole, scale_field, scale_triad):
    groups, planes, rows, lanes = share.shape
    vmem = pl.BlockSpec(memory_space=pltpu.VMEM)
    return pl.pallas_call(
        functools.partial(finish_kernel, scale_field, scale_triad),
        out_shape=(
            jax.ShapeDtypeStruct((groups * rows, planes, lanes), jnp.float32),
            jax.ShapeDtypeStruct((2, FBLK, FBLK), jnp.float32),
        ),
        in_specs=[vmem, vmem],
        out_specs=(vmem, vmem),
        compiler_params=pltpu.CompilerParams(vmem_limit_bytes=4 << 20),
    )(share, whole)


def per_device(velocity_modes, block_list, counts):
    blocks_here, _, _, freq_count, planes, cross_cells = velocity_modes.shape
    welch_all = blocks_here * lax.axis_size("blk")
    cells_all = planes * lax.axis_size("cell") * cross_cells
    scale_field = -0.5 * 0.25 / math.sqrt(welch_all * FBLK)
    scale_triad = -0.5 * 0.25 / math.sqrt(welch_all * cells_all)

    modes = velocity_modes.reshape(blocks_here, 6, freq_count, planes, cross_cells).swapaxes(2, 3)
    low_planes, high_planes = (
        jnp.stack(
            [lax.dynamic_slice_in_dim(modes[:, :, p], block_list[n, 1] * FBLK, FBLK, 2) for n in range(2)]
        )
        for p in (0, planes - 1)
    )
    count = lax.axis_size("cell")
    below = lax.ppermute(high_planes, "cell", [(i, i + 1) for i in range(count - 1)])
    above = lax.ppermute(low_planes, "cell", [(i + 1, i) for i in range(count - 1)])

    field, sums = run_triads(block_list, counts, modes, below, above)
    share, triads = exchange(field, sums)
    return finish(share, triads, scale_field, scale_triad)


def solution(mesh):
    return jax.shard_map(
        per_device,
        mesh=mesh,
        in_specs=(P("blk", None, None, None, "cell", None), P(), P()),
        out_specs=(P("blk", "cell", None), P()),
        check_vma=False,
    )
```

```python
import functools
import math

import jax
import jax.numpy as jnp
from jax import lax
from jax.experimental import pallas as pl
from jax.experimental.pallas import tpu as pltpu
from jax.sharding import PartitionSpec as P

FBLK = 64
CZ = 16
CORES = 2
DEPTH = 8


def slot_spread(parts):
    slot = lax.broadcasted_iota(jnp.int32, parts[0].shape, 1) // CZ
    for k in (1, 2, 4):
        odd = slot & k != 0
        parts = [jnp.where(odd, parts[(e + k) % 8], parts[e]) for e in range(8)]
    return [parts[-y % 8] for y in range(8)]


def slot_transpose(parts):
    width = parts[0].shape[1]
    turned = [parts[0]] + [pltpu.roll(parts[s], CZ * s, 1) for s in range(1, 8)]
    mixed = slot_spread(turned)
    return [mixed[0]] + [pltpu.roll(mixed[y], width - CZ * y, 1) for y in range(1, 8)]


def row_sums(parts):
    row = lax.broadcasted_iota(jnp.int32, parts[0].shape, 0)
    parts = list(parts)
    for k in (4, 2, 1):
        keep = row & k == 0
        merged = []
        for a in range(k):
            first, second = parts[a], parts[a + k]
            other = jnp.where(keep, second, first)
            if k == 4:
                other = pltpu.roll(other, 4, 0)
            else:
                other = jnp.where(keep, pltpu.roll(other, 8 - k, 0), pltpu.roll(other, k, 0))
            merged.append(jnp.where(keep, first, second) + other)
        parts = merged
    return parts[0]


def regroup_kernel(modes_ref, grouped, packed):
    def regroup(index, _):
        i = index % 3
        b = index // 3
        for p in range(4):
            for block in range(4):
                parts = []
                for v in range(8):
                    rows = pl.ds(block * FBLK + 8 * v, 8)
                    parts.append(
                        jnp.concatenate(
                            [modes_ref[b, 2 * i, p, rows, :], modes_ref[b, 2 * i + 1, p, rows, :]], axis=0
                        )
                    )
                parts = slot_transpose(parts)
                for y in range(8):
                    packed[b, 8 * p + y, i, block] = parts[y]
                    grouped[b, 8 * p + y, i, block] = parts[y].astype(jnp.float32)
        return 0

    lax.fori_loop(0, 6, regroup, 0)


def triad_kernel(
    list_ref,
    count_ref,
    modes_ref,
    below_ref,
    above_ref,
    grouped,
    packed,
    field_ref,
    sums_ref,
    left_a,
    left_b,
    right_a,
    right_b,
    window_a,
    window_b,
    pair_sums,
    rows_out,
    triads,
):
    lefts, rights, windows = (left_a, left_b), (right_a, right_b), (window_a, window_b)
    lanes = modes_ref.shape[4]
    field_ref[...] = jnp.zeros_like(field_ref)
    right_a[...] = jnp.zeros_like(right_a)
    right_b[...] = jnp.zeros_like(right_b)

    lane = lax.broadcasted_iota(jnp.int32, (16, lanes), 1)
    row = lax.broadcasted_iota(jnp.int32, (16, lanes), 0)
    z = lane % CZ
    slot = lane // CZ
    slot8 = lax.broadcasted_iota(jnp.int32, (8, lanes), 1) // CZ
    row8 = lax.broadcasted_iota(jnp.int32, (8, lanes), 0)
    picked = (slot8 == row8).astype(jnp.float32)
    zero = jnp.zeros((16, lanes), jnp.bfloat16)

    def fill_left(plane, index, left):
        n = plane // 4
        p = plane % 4
        at_l = list_ref[n, 1]
        i = index % 3
        b = index // 3
        for cc in range(4):
            first = pl.multiple_of(at_l * FBLK + cc * 16, 16)
            own = pl.ds(cc * 16, 16)
            shifted = []
            for part in range(2):
                comp = 2 * i + part
                u = modes_ref[b, comp, p, pl.ds(first, 16), :]
                up = modes_ref[b, comp, jnp.minimum(p + 1, 3), pl.ds(first, 16), :]
                down = modes_ref[b, comp, jnp.maximum(p - 1, 0), pl.ds(first, 16), :]
                up = jnp.where(p == 3, above_ref[n, b, comp, own, :], up)
                down = jnp.where(p == 0, below_ref[n, b, comp, own, :], down)
                shifted.append(
                    slot_spread(
                        [
                            up,
                            pltpu.roll(-down, CZ, 1),
                            jnp.where(slot == 1, zero, pltpu.roll(u, CZ, 1)),
                            jnp.where(slot == 3, zero, pltpu.roll(-u, 4 * CZ, 1)),
                            jnp.where(z == CZ - 1, zero, pltpu.roll(u, 4 * CZ - 1, 1)),
                            jnp.where(z == 0, zero, pltpu.roll(-u, 5 * CZ + 1, 1)),
                            zero,
                            zero,
                        ]
                    )
                )
            at = pl.multiple_of((cc * 3 + i) * 32, 32)
            for y in range(8):
                real = shifted[0][y]
                imag = shifted[1][y]
                left[b, y, pl.ds(at, 16), :lanes] = real
                left[b, y, pl.ds(at, 16), lanes:] = -imag
                left[b, y, pl.ds(at + 16, 16), :lanes] = imag
                left[b, y, pl.ds(at + 16, 16), lanes:] = real

    def build(step, right, window):
        n = step // 32
        group = step % 32
        at_k = list_ref[n, 0]
        at_m = at_k + list_ref[n, 1]
        y = group % 8
        for b in range(2):
            for i in range(3):
                now = packed[b, group, i, at_m]
                later = packed[b, group, i, at_m + 1]
                for g in range(9):
                    turned = now if g == 0 else later
                    if 0 < g < 8:
                        turned = pltpu.roll(jnp.where(slot >= g, now, later), lanes - CZ * g, 1)
                    turned = turned.astype(jnp.float32)
                    for part in range(2):
                        window[b, 2 * i + part, 8 * g : 8 * g + 8, :] = turned[8 * part : 8 * part + 8]
                for part in range(2):
                    for a in range(8):
                        donor = grouped[b, group, i, at_k, pl.ds(8 * part + a, 16, stride=0), :]
                        spread = jnp.where(z == row, donor, 0.0).astype(jnp.bfloat16)
                        for side in range(2):
                            top = pl.multiple_of(part * lanes + (y + 2 * i + side) % 8 * 16, 16)
                            right[b, pl.ds(top, 16), a * lanes : (a + 1) * lanes] = spread

    def contract(y, live, left, right, window):
        kept_all = []
        for a2 in range(4):
            products = [
                jnp.dot(
                    left[b, y],
                    right[b, :, a2 * 2 * lanes : (a2 + 1) * 2 * lanes],
                    preferred_element_type=jnp.float32,
                )
                for b in range(2)
            ]
            for half in range(2):
                a = 2 * a2 + half
                kept = None
                for ch in range(FBLK // 8):
                    total = None
                    for b in range(2):
                        for comp in range(6):
                            at = (ch // 2 * 6 + comp) * 16 + 8 * (ch % 2)
                            term = (
                                products[b][at : at + 8, half * lanes : (half + 1) * lanes]
                                * window[b, comp, 8 * ch + a : 8 * ch + a + 8, :]
                            )
                            total = term if total is None else total + term
                    pair_sums[a, 8 * ch : 8 * ch + 8, :] += total
                    masked = jnp.where(row8 < live - 8 * ch, total, 0.0)
                    kept = masked if kept is None else kept + masked
                kept_all.append(kept)
        rows_out[y] = row_sums(kept_all)

    lax.fori_loop(0, 6, lambda index, _: (fill_left(0, index, left_a), 0)[1], 0)
    build(0, right_a, window_a)

    def plane_pair(t, _):
        n = t // 2
        at_k = list_ref[n, 0]
        live = count_ref[n]

        @pl.when(t % 2 == 0)
        def _():
            pair_sums[...] = jnp.zeros_like(pair_sums)

        for parity in range(2):
            plane = 2 * t + parity

            def group_pair(y2, _):
                for half in range(4):
                    y = 4 * y2 + half
                    contract(y, live, lefts[parity], rights[half % 2], windows[half % 2])
                    build(jnp.minimum(plane * 8 + y + 1, 63), rights[1 - half % 2], windows[1 - half % 2])
                    fill_left(jnp.minimum(plane + 1, 7), jnp.minimum(y, 5), lefts[1 - parity])
                return 0

            lax.fori_loop(0, 2, group_pair, 0)
            parts = slot_transpose([rows_out[y] for y in range(8)])
            for v in range(8):
                field_ref[at_k * 8 + v, plane % 4] += parts[v]

        @pl.when(t % 2 == 1)
        def _():
            for a in range(8):
                triads[n, pl.ds(a, 8, stride=8), :] = lax.dot_general(
                    picked,
                    pair_sums[a],
                    (((1,), (1,)), ((), ())),
                    precision=lax.Precision.HIGHEST,
                    preferred_element_type=jnp.float32,
                )

        return 0

    lax.fori_loop(0, 4, plane_pair, 0)
    column = lax.broadcasted_iota(jnp.int32, (FBLK, FBLK), 1)
    for n in range(2):
        sums_ref[:, n * FBLK : (n + 1) * FBLK] = jnp.where(column < count_ref[n], triads[n], 0.0)


def run_regroup(modes):
    lanes = modes.shape[4]
    vmem = pl.BlockSpec(memory_space=pltpu.VMEM)
    shape = (2, 32, 3, 4, 16, lanes)
    return pl.pallas_call(
        regroup_kernel,
        out_shape=(jax.ShapeDtypeStruct(shape, jnp.float32), jax.ShapeDtypeStruct(shape, jnp.bfloat16)),
        in_specs=[vmem],
        out_specs=(vmem, vmem),
        compiler_params=pltpu.CompilerParams(vmem_limit_bytes=16 << 20),
        cost_estimate=pl.CostEstimate(flops=40_000_000, bytes_accessed=13_000_000, transcendentals=0),
    )(modes)


def run_triads(block_list, counts, modes, below, above):
    grouped, packed = run_regroup(modes)
    planes, freq_count, cross_cells = modes.shape[2:]
    donors_span = (freq_count // FBLK - 1) * FBLK
    vmem = pl.BlockSpec(memory_space=pltpu.VMEM)
    smem = pl.BlockSpec(memory_space=pltpu.SMEM)
    return pl.pallas_call(
        triad_kernel,
        out_shape=(
            jax.ShapeDtypeStruct((donors_span // 8, planes, 8, cross_cells), jnp.float32),
            jax.ShapeDtypeStruct((FBLK, 2 * FBLK), jnp.float32),
        ),
        in_specs=[smem, smem, vmem, vmem, vmem, vmem, vmem],
        out_specs=(vmem, vmem),
        scratch_shapes=[
            pltpu.VMEM((2, 8, 384, 2 * cross_cells), jnp.bfloat16),
            pltpu.VMEM((2, 8, 384, 2 * cross_cells), jnp.bfloat16),
            pltpu.VMEM((2, 2 * cross_cells, 8 * cross_cells), jnp.bfloat16),
            pltpu.VMEM((2, 2 * cross_cells, 8 * cross_cells), jnp.bfloat16),
            pltpu.VMEM((2, 6, 72, cross_cells), jnp.float32),
            pltpu.VMEM((2, 6, 72, cross_cells), jnp.float32),
            pltpu.VMEM((8, FBLK, cross_cells), jnp.float32),
            pltpu.VMEM((8, 8, cross_cells), jnp.float32),
            pltpu.VMEM((2, FBLK, FBLK), jnp.float32),
        ],
        compiler_params=pltpu.CompilerParams(vmem_limit_bytes=32 << 20),
    )(block_list, counts, modes, below, above, grouped, packed)


def exchange_kernel(
    field_ref,
    sums_ref,
    share_ref,
    whole_ref,
    field_in,
    part_in,
    x_in,
    z_in,
    whole,
    sent,
    field_got,
    part_got,
    x_got,
    z_got,
    whole_got,
):
    cell = lax.axis_index("cell")
    blk = lax.axis_index("blk")
    blks = field_ref.shape[0]
    owners = CORES * blks
    part = sums_ref.shape[0] // owners
    depth = z_in.shape[0]
    far = x_in.shape[0]
    near = depth * CORES
    core = lax.rem(cell, CORES)
    z_at = lax.rem(cell // CORES, depth)
    x_at = cell // near
    owner = blk * CORES + core
    mesh_id = pl.DeviceIdType.MESH

    def blk_peer(step):
        return (cell, lax.rem(blk + step, blks))

    def owner_peer(step):
        other = lax.rem(owner + step, owners)
        return (cell - core + lax.rem(other, CORES), other // CORES)

    def x_peer(step):
        return (lax.rem(x_at + step, far) * near + z_at * CORES + core, blk)

    def z_peer(step):
        return (x_at * near + lax.rem(z_at + step, depth) * CORES + core, blk)

    barrier = pltpu.get_barrier_semaphore()
    peers = [owner_peer(s) for s in range(1, owners)]
    peers += [x_peer(s) for s in range(1, far)]
    peers += [z_peer(s) for s in range(1, depth)]
    for peer in peers:
        pl.semaphore_signal(barrier, inc=1, device_id=peer, device_id_type=mesh_id)
    pl.semaphore_wait(barrier, len(peers))

    copies = []

    def send(source, target, got, peer):
        copy = pltpu.make_async_remote_copy(
            src_ref=source,
            dst_ref=target,
            send_sem=sent.at[len(copies)],
            recv_sem=got,
            device_id=peer,
            device_id_type=mesh_id,
        )
        copy.start()
        copies.append(copy)
        return copy

    def rows_of(at):
        return pl.ds(pl.multiple_of(at * part, part), part)

    first = []
    for s in range(1, owners):
        rows = rows_of(lax.rem(owner + s, owners))
        first.append(send(sums_ref.at[rows], part_in.at[s - 1], part_got.at[s - 1], owner_peer(s)))
    fields = []
    for s in range(1, blks):
        fields.append(
            send(field_ref.at[lax.rem(blk + s, blks)], field_in.at[s - 1], field_got.at[s - 1], blk_peer(s))
        )
    for copy in first:
        copy.wait_recv()
    total = sums_ref[rows_of(owner), :]
    for s in range(1, owners):
        total = total + part_in[s - 1]
    x_in[x_at] = total
    second = [send(x_in.at[x_at], x_in.at[x_at], x_got.at[s - 1], x_peer(s)) for s in range(1, far)]
    for copy in second:
        copy.wait_recv()
    total = x_in[0]
    for k in range(1, far):
        total = total + x_in[k]
    z_in[z_at] = total
    third = [send(z_in.at[z_at], z_in.at[z_at], z_got.at[s - 1], z_peer(s)) for s in range(1, depth)]
    for copy in third:
        copy.wait_recv()
    total = z_in[0]
    for k in range(1, depth):
        total = total + z_in[k]
    whole[rows_of(owner), :] = total
    fourth = [
        send(whole.at[rows_of(owner)], whole.at[rows_of(owner)], whole_got.at[s - 1], owner_peer(s))
        for s in range(1, owners)
    ]
    for copy in fields:
        copy.wait_recv()
    share = field_ref[blk]
    for s in range(1, blks):
        share = share + field_in[s - 1]
    share_ref[...] = share
    for copy in fourth:
        copy.wait_recv()
    whole_ref[...] = whole[...]
    for copy in copies:
        copy.wait_send()


def exchange(local_field, sums):
    blks = lax.axis_size("blk")
    owners = CORES * blks
    far = lax.axis_size("cell") // (DEPTH * CORES)
    share = local_field.shape[0] // blks
    chunks = local_field.reshape(blks, share, *local_field.shape[1:])
    part = sums.shape[0] // owners
    lanes = sums.shape[1]
    vmem = pl.BlockSpec(memory_space=pltpu.VMEM)
    dma = pltpu.SemaphoreType.DMA
    sends = 2 * (owners - 1) + (blks - 1) + (far - 1) + (DEPTH - 1)
    return pl.pallas_call(
        exchange_kernel,
        out_shape=(
            jax.ShapeDtypeStruct(chunks.shape[1:], jnp.float32),
            jax.ShapeDtypeStruct(sums.shape, jnp.float32),
        ),
        in_specs=[vmem, vmem],
        out_specs=(vmem, vmem),
        scratch_shapes=[
            pltpu.VMEM((blks - 1,) + chunks.shape[1:], jnp.float32),
            pltpu.VMEM((owners - 1, part, lanes), jnp.float32),
            pltpu.VMEM((far, part, lanes), jnp.float32),
            pltpu.VMEM((DEPTH, part, lanes), jnp.float32),
            pltpu.VMEM(sums.shape, jnp.float32),
            dma((sends,)),
            dma((blks - 1,)),
            dma((owners - 1,)),
            dma((far - 1,)),
            dma((DEPTH - 1,)),
            dma((owners - 1,)),
        ],
        compiler_params=pltpu.CompilerParams(collective_id=0, has_side_effects=True, vmem_limit_bytes=4 << 20),
    )(chunks, sums)


def cut_kernel(list_ref, modes_ref, low_ref, high_ref):
    last = modes_ref.shape[2] - 1
    for n in range(2):
        rows = pl.ds(pl.multiple_of(list_ref[n, 1] * FBLK, FBLK), FBLK)
        low_ref[n] = modes_ref[:, :, 0, rows, :]
        high_ref[n] = modes_ref[:, :, last, rows, :]


def cut(block_list, modes):
    blocks, comps, _, _, lanes = modes.shape
    vmem = pl.BlockSpec(memory_space=pltpu.VMEM)
    side = jax.ShapeDtypeStruct((2, blocks, comps, FBLK, lanes), jnp.bfloat16)
    return pl.pallas_call(
        cut_kernel,
        out_shape=(side, side),
        in_specs=[pl.BlockSpec(memory_space=pltpu.SMEM), vmem],
        out_specs=(vmem, vmem),
        compiler_params=pltpu.CompilerParams(vmem_limit_bytes=8 << 20),
    )(block_list, modes)


def finish_kernel(scale_field, scale_triad, share_ref, whole_ref, transfer_ref, triad_ref):
    groups, planes = share_ref.shape[:2]
    for g in range(groups):
        for p in range(planes):
            transfer_ref[8 * g : 8 * g + 8, p, :] = share_ref[g, p] * scale_field
    for n in range(2):
        triad_ref[n] = whole_ref[:, n * FBLK : (n + 1) * FBLK] * scale_triad


def finish(share, whole, scale_field, scale_triad):
    groups, planes, rows, lanes = share.shape
    vmem = pl.BlockSpec(memory_space=pltpu.VMEM)
    return pl.pallas_call(
        functools.partial(finish_kernel, scale_field, scale_triad),
        out_shape=(
            jax.ShapeDtypeStruct((groups * rows, planes, lanes), jnp.float32),
            jax.ShapeDtypeStruct((2, FBLK, FBLK), jnp.float32),
        ),
        in_specs=[vmem, vmem],
        out_specs=(vmem, vmem),
        compiler_params=pltpu.CompilerParams(vmem_limit_bytes=4 << 20),
    )(share, whole)


def per_device(velocity_modes, block_list, counts):
    blocks_here, _, _, freq_count, planes, cross_cells = velocity_modes.shape
    welch_all = blocks_here * lax.axis_size("blk")
    cells_all = planes * lax.axis_size("cell") * cross_cells
    scale_field = -0.5 * 0.25 / math.sqrt(welch_all * FBLK)
    scale_triad = -0.5 * 0.25 / math.sqrt(welch_all * cells_all)

    modes = velocity_modes.reshape(blocks_here, 6, freq_count, planes, cross_cells).swapaxes(2, 3)
    low_planes, high_planes = cut(block_list, modes)
    count = lax.axis_size("cell")
    below = lax.ppermute(high_planes, "cell", [(i, i + 1) for i in range(count - 1)])
    above = lax.ppermute(low_planes, "cell", [(i + 1, i) for i in range(count - 1)])

    field, sums = run_triads(block_list, counts, modes, below, above)
    share, triads = exchange(field, sums)
    return finish(share, triads, scale_field, scale_triad)


def solution(mesh):
    return jax.shard_map(
        per_device,
        mesh=mesh,
        in_specs=(P("blk", None, None, None, "cell", None), P(), P()),
        out_specs=(P("blk", "cell", None), P()),
        check_vma=False,
    )
```

```python
import functools
import math

import jax
import jax.numpy as jnp
from jax import lax
from jax.experimental import pallas as pl
from jax.experimental.pallas import tpu as pltpu
from jax.sharding import PartitionSpec as P

FBLK = 64
CZ = 16
CORES = 2
DEPTH = 8


def slot_spread(parts):
    slot = lax.broadcasted_iota(jnp.int32, parts[0].shape, 1) // CZ
    for k in (1, 2, 4):
        odd = slot & k != 0
        parts = [jnp.where(odd, parts[(e + k) % 8], parts[e]) for e in range(8)]
    return [parts[-y % 8] for y in range(8)]


def slot_transpose(parts):
    width = parts[0].shape[1]
    turned = [parts[0]] + [pltpu.roll(parts[s], CZ * s, 1) for s in range(1, 8)]
    mixed = slot_spread(turned)
    return [mixed[0]] + [pltpu.roll(mixed[y], width - CZ * y, 1) for y in range(1, 8)]


def row_sums(parts):
    row = lax.broadcasted_iota(jnp.int32, parts[0].shape, 0)
    parts = list(parts)
    for k in (4, 2, 1):
        keep = row & k == 0
        merged = []
        for a in range(k):
            first, second = parts[a], parts[a + k]
            other = jnp.where(keep, second, first)
            if k == 4:
                other = pltpu.roll(other, 4, 0)
            else:
                other = jnp.where(keep, pltpu.roll(other, 8 - k, 0), pltpu.roll(other, k, 0))
            merged.append(jnp.where(keep, first, second) + other)
        parts = merged
    return parts[0]


def regroup_kernel(modes_ref, low_ref, high_ref, grouped, packed, below_ref, above_ref, sent, got):
    cells = lax.axis_size("cell")
    cell = lax.axis_index("cell")
    blk = lax.axis_index("blk")
    mesh_id = pl.DeviceIdType.MESH
    up = (lax.rem(cell + 1, cells), blk)
    down = (lax.rem(cell + cells - 1, cells), blk)
    barrier = pltpu.get_barrier_semaphore()
    for peer in (up, down):
        pl.semaphore_signal(barrier, inc=1, device_id=peer, device_id_type=mesh_id)
    pl.semaphore_wait(barrier, 2)
    copies = [
        pltpu.make_async_remote_copy(
            src_ref=source,
            dst_ref=target,
            send_sem=sent.at[k],
            recv_sem=got.at[k],
            device_id=peer,
            device_id_type=mesh_id,
        )
        for k, (source, target, peer) in enumerate([(high_ref, below_ref, up), (low_ref, above_ref, down)])
    ]
    for copy in copies:
        copy.start()

    def regroup(index, _):
        p = index % 4
        i = index // 4 % 3
        b = index // 12
        for block in range(4):
            parts = []
            for v in range(8):
                rows = pl.ds(block * FBLK + 8 * v, 8)
                parts.append(
                    jnp.concatenate(
                        [modes_ref[b, 2 * i, p, rows, :], modes_ref[b, 2 * i + 1, p, rows, :]], axis=0
                    )
                )
            parts = slot_transpose(parts)
            for y in range(8):
                packed[b, 8 * p + y, i, block] = parts[y]
                grouped[b, 8 * p + y, i, block] = parts[y].astype(jnp.float32)
        return 0

    lax.fori_loop(0, 24, regroup, 0)
    for copy in copies:
        copy.wait()

    @pl.when(cell == 0)
    def _():
        below_ref[...] = jnp.zeros_like(below_ref)

    @pl.when(cell == cells - 1)
    def _():
        above_ref[...] = jnp.zeros_like(above_ref)


def triad_kernel(
    list_ref,
    count_ref,
    modes_ref,
    below_ref,
    above_ref,
    grouped,
    packed,
    field_ref,
    sums_ref,
    left_a,
    left_b,
    right_a,
    right_b,
    window_a,
    window_b,
    pair_sums,
    rows_out,
    triads,
):
    lefts, rights, windows = (left_a, left_b), (right_a, right_b), (window_a, window_b)
    lanes = modes_ref.shape[4]
    field_ref[...] = jnp.zeros_like(field_ref)
    right_a[...] = jnp.zeros_like(right_a)
    right_b[...] = jnp.zeros_like(right_b)

    lane = lax.broadcasted_iota(jnp.int32, (16, lanes), 1)
    row = lax.broadcasted_iota(jnp.int32, (16, lanes), 0)
    z = lane % CZ
    slot = lane // CZ
    slot8 = lax.broadcasted_iota(jnp.int32, (8, lanes), 1) // CZ
    row8 = lax.broadcasted_iota(jnp.int32, (8, lanes), 0)
    picked = (slot8 == row8).astype(jnp.float32)
    zero = jnp.zeros((16, lanes), jnp.bfloat16)

    def fill_left(plane, index, left):
        n = plane // 4
        p = plane % 4
        at_l = list_ref[n, 1]
        i = index % 3
        b = index // 3
        for cc in range(4):
            first = pl.multiple_of(at_l * FBLK + cc * 16, 16)
            own = pl.ds(cc * 16, 16)
            shifted = []
            for part in range(2):
                comp = 2 * i + part
                u = modes_ref[b, comp, p, pl.ds(first, 16), :]
                up = modes_ref[b, comp, jnp.minimum(p + 1, 3), pl.ds(first, 16), :]
                down = modes_ref[b, comp, jnp.maximum(p - 1, 0), pl.ds(first, 16), :]
                up = jnp.where(p == 3, above_ref[n, b, comp, own, :], up)
                down = jnp.where(p == 0, below_ref[n, b, comp, own, :], down)
                shifted.append(
                    slot_spread(
                        [
                            up,
                            pltpu.roll(-down, CZ, 1),
                            jnp.where(slot == 1, zero, pltpu.roll(u, CZ, 1)),
                            jnp.where(slot == 3, zero, pltpu.roll(-u, 4 * CZ, 1)),
                            jnp.where(z == CZ - 1, zero, pltpu.roll(u, 4 * CZ - 1, 1)),
                            jnp.where(z == 0, zero, pltpu.roll(-u, 5 * CZ + 1, 1)),
                            zero,
                            zero,
                        ]
                    )
                )
            at = pl.multiple_of((cc * 3 + i) * 32, 32)
            for y in range(8):
                real = shifted[0][y]
                imag = shifted[1][y]
                left[b, y, pl.ds(at, 16), :lanes] = real
                left[b, y, pl.ds(at, 16), lanes:] = -imag
                left[b, y, pl.ds(at + 16, 16), :lanes] = imag
                left[b, y, pl.ds(at + 16, 16), lanes:] = real

    def build(step, right, window):
        n = step // 32
        group = step % 32
        at_k = list_ref[n, 0]
        at_m = at_k + list_ref[n, 1]
        y = group % 8
        for b in range(2):
            for i in range(3):
                now = packed[b, group, i, at_m]
                later = packed[b, group, i, at_m + 1]
                for g in range(9):
                    turned = now if g == 0 else later
                    if 0 < g < 8:
                        turned = pltpu.roll(jnp.where(slot >= g, now, later), lanes - CZ * g, 1)
                    turned = turned.astype(jnp.float32)
                    for part in range(2):
                        window[b, 2 * i + part, 8 * g : 8 * g + 8, :] = turned[8 * part : 8 * part + 8]
                for part in range(2):
                    for a in range(8):
                        donor = grouped[b, group, i, at_k, pl.ds(8 * part + a, 16, stride=0), :]
                        spread = jnp.where(z == row, donor, 0.0).astype(jnp.bfloat16)
                        for side in range(2):
                            top = pl.multiple_of(part * lanes + (y + 2 * i + side) % 8 * 16, 16)
                            right[b, pl.ds(top, 16), a * lanes : (a + 1) * lanes] = spread

    def contract(y, live, left, right, window):
        kept_all = []
        for a2 in range(4):
            products = [
                jnp.dot(
                    left[b, y],
                    right[b, :, a2 * 2 * lanes : (a2 + 1) * 2 * lanes],
                    preferred_element_type=jnp.float32,
                )
                for b in range(2)
            ]
            for half in range(2):
                a = 2 * a2 + half
                kept = None
                for ch in range(FBLK // 8):
                    total = None
                    for b in range(2):
                        for comp in range(6):
                            at = (ch // 2 * 6 + comp) * 16 + 8 * (ch % 2)
                            term = (
                                products[b][at : at + 8, half * lanes : (half + 1) * lanes]
                                * window[b, comp, 8 * ch + a : 8 * ch + a + 8, :]
                            )
                            total = term if total is None else total + term
                    pair_sums[a, 8 * ch : 8 * ch + 8, :] += total
                    masked = jnp.where(row8 < live - 8 * ch, total, 0.0)
                    kept = masked if kept is None else kept + masked
                kept_all.append(kept)
        rows_out[y] = row_sums(kept_all)

    lax.fori_loop(0, 6, lambda index, _: (fill_left(0, index, left_a), 0)[1], 0)
    build(0, right_a, window_a)

    def plane_pair(t, _):
        n = t // 2
        at_k = list_ref[n, 0]
        live = count_ref[n]

        @pl.when(t % 2 == 0)
        def _():
            pair_sums[...] = jnp.zeros_like(pair_sums)

        for parity in range(2):
            plane = 2 * t + parity

            def group_pair(y2, _):
                for half in range(4):
                    y = 4 * y2 + half
                    contract(y, live, lefts[parity], rights[half % 2], windows[half % 2])
                    build(jnp.minimum(plane * 8 + y + 1, 63), rights[1 - half % 2], windows[1 - half % 2])
                    fill_left(jnp.minimum(plane + 1, 7), jnp.minimum(y, 5), lefts[1 - parity])
                return 0

            lax.fori_loop(0, 2, group_pair, 0)
            parts = slot_transpose([rows_out[y] for y in range(8)])
            for v in range(8):
                field_ref[at_k * 8 + v, plane % 4] += parts[v]

        @pl.when(t % 2 == 1)
        def _():
            for a in range(8):
                triads[n, pl.ds(a, 8, stride=8), :] = lax.dot_general(
                    picked,
                    pair_sums[a],
                    (((1,), (1,)), ((), ())),
                    precision=lax.Precision.HIGHEST,
                    preferred_element_type=jnp.float32,
                )

        return 0

    lax.fori_loop(0, 4, plane_pair, 0)
    column = lax.broadcasted_iota(jnp.int32, (FBLK, FBLK), 1)
    for n in range(2):
        sums_ref[:, n * FBLK : (n + 1) * FBLK] = jnp.where(column < count_ref[n], triads[n], 0.0)


def run_regroup(modes, low_planes, high_planes):
    lanes = modes.shape[4]
    vmem = pl.BlockSpec(memory_space=pltpu.VMEM)
    shape = (2, 32, 3, 4, 16, lanes)
    side = jax.ShapeDtypeStruct(low_planes.shape, low_planes.dtype)
    return pl.pallas_call(
        regroup_kernel,
        out_shape=(jax.ShapeDtypeStruct(shape, jnp.float32), jax.ShapeDtypeStruct(shape, jnp.bfloat16), side, side),
        in_specs=[vmem] * 3,
        out_specs=(vmem,) * 4,
        scratch_shapes=[pltpu.SemaphoreType.DMA((2,)), pltpu.SemaphoreType.DMA((2,))],
        compiler_params=pltpu.CompilerParams(collective_id=1, has_side_effects=True, vmem_limit_bytes=16 << 20),
    )(modes, low_planes, high_planes)


def run_triads(block_list, counts, modes, below, above, grouped, packed):
    planes, freq_count, cross_cells = modes.shape[2:]
    donors_span = (freq_count // FBLK - 1) * FBLK
    vmem = pl.BlockSpec(memory_space=pltpu.VMEM)
    smem = pl.BlockSpec(memory_space=pltpu.SMEM)
    return pl.pallas_call(
        triad_kernel,
        out_shape=(
            jax.ShapeDtypeStruct((donors_span // 8, planes, 8, cross_cells), jnp.float32),
            jax.ShapeDtypeStruct((FBLK, 2 * FBLK), jnp.float32),
        ),
        in_specs=[smem, smem, vmem, vmem, vmem, vmem, vmem],
        out_specs=(vmem, vmem),
        scratch_shapes=[
            pltpu.VMEM((2, 8, 384, 2 * cross_cells), jnp.bfloat16),
            pltpu.VMEM((2, 8, 384, 2 * cross_cells), jnp.bfloat16),
            pltpu.VMEM((2, 2 * cross_cells, 8 * cross_cells), jnp.bfloat16),
            pltpu.VMEM((2, 2 * cross_cells, 8 * cross_cells), jnp.bfloat16),
            pltpu.VMEM((2, 6, 72, cross_cells), jnp.float32),
            pltpu.VMEM((2, 6, 72, cross_cells), jnp.float32),
            pltpu.VMEM((8, FBLK, cross_cells), jnp.float32),
            pltpu.VMEM((8, 8, cross_cells), jnp.float32),
            pltpu.VMEM((2, FBLK, FBLK), jnp.float32),
        ],
        compiler_params=pltpu.CompilerParams(vmem_limit_bytes=32 << 20),
    )(block_list, counts, modes, below, above, grouped, packed)


def exchange_kernel(
    field_ref,
    sums_ref,
    share_ref,
    whole_ref,
    field_in,
    part_in,
    x_in,
    z_in,
    whole,
    sent,
    field_got,
    part_got,
    x_got,
    z_got,
    whole_got,
):
    cell = lax.axis_index("cell")
    blk = lax.axis_index("blk")
    blks = field_ref.shape[0]
    owners = CORES * blks
    part = sums_ref.shape[0] // owners
    depth = z_in.shape[0]
    far = x_in.shape[0]
    near = depth * CORES
    core = lax.rem(cell, CORES)
    z_at = lax.rem(cell // CORES, depth)
    x_at = cell // near
    owner = blk * CORES + core
    mesh_id = pl.DeviceIdType.MESH

    def blk_peer(step):
        return (cell, lax.rem(blk + step, blks))

    def owner_peer(step):
        other = lax.rem(owner + step, owners)
        return (cell - core + lax.rem(other, CORES), other // CORES)

    def x_peer(step):
        return (lax.rem(x_at + step, far) * near + z_at * CORES + core, blk)

    def z_peer(step):
        return (x_at * near + lax.rem(z_at + step, depth) * CORES + core, blk)

    barrier = pltpu.get_barrier_semaphore()
    peers = [owner_peer(s) for s in range(1, owners)]
    peers += [x_peer(s) for s in range(1, far)]
    peers += [z_peer(s) for s in range(1, depth)]
    for peer in peers:
        pl.semaphore_signal(barrier, inc=1, device_id=peer, device_id_type=mesh_id)
    pl.semaphore_wait(barrier, len(peers))

    copies = []

    def send(source, target, got, peer):
        copy = pltpu.make_async_remote_copy(
            src_ref=source,
            dst_ref=target,
            send_sem=sent.at[len(copies)],
            recv_sem=got,
            device_id=peer,
            device_id_type=mesh_id,
        )
        copy.start()
        copies.append(copy)
        return copy

    def rows_of(at):
        return pl.ds(pl.multiple_of(at * part, part), part)

    first = []
    for s in range(1, owners):
        rows = rows_of(lax.rem(owner + s, owners))
        first.append(send(sums_ref.at[rows], part_in.at[s - 1], part_got.at[s - 1], owner_peer(s)))
    fields = []
    for s in range(1, blks):
        fields.append(
            send(field_ref.at[lax.rem(blk + s, blks)], field_in.at[s - 1], field_got.at[s - 1], blk_peer(s))
        )
    for copy in first:
        copy.wait_recv()
    total = sums_ref[rows_of(owner), :]
    for s in range(1, owners):
        total = total + part_in[s - 1]
    x_in[x_at] = total
    second = [send(x_in.at[x_at], x_in.at[x_at], x_got.at[s - 1], x_peer(s)) for s in range(1, far)]
    for copy in second:
        copy.wait_recv()
    total = x_in[0]
    for k in range(1, far):
        total = total + x_in[k]
    z_in[z_at] = total
    third = [send(z_in.at[z_at], z_in.at[z_at], z_got.at[s - 1], z_peer(s)) for s in range(1, depth)]
    for copy in third:
        copy.wait_recv()
    total = z_in[0]
    for k in range(1, depth):
        total = total + z_in[k]
    whole[rows_of(owner), :] = total
    fourth = [
        send(whole.at[rows_of(owner)], whole.at[rows_of(owner)], whole_got.at[s - 1], owner_peer(s))
        for s in range(1, owners)
    ]
    for copy in fields:
        copy.wait_recv()
    share = field_ref[blk]
    for s in range(1, blks):
        share = share + field_in[s - 1]
    share_ref[...] = share
    for copy in fourth:
        copy.wait_recv()
    whole_ref[...] = whole[...]
    for copy in copies:
        copy.wait_send()


def exchange(local_field, sums):
    blks = lax.axis_size("blk")
    owners = CORES * blks
    far = lax.axis_size("cell") // (DEPTH * CORES)
    share = local_field.shape[0] // blks
    chunks = local_field.reshape(blks, share, *local_field.shape[1:])
    part = sums.shape[0] // owners
    lanes = sums.shape[1]
    vmem = pl.BlockSpec(memory_space=pltpu.VMEM)
    dma = pltpu.SemaphoreType.DMA
    sends = 2 * (owners - 1) + (blks - 1) + (far - 1) + (DEPTH - 1)
    return pl.pallas_call(
        exchange_kernel,
        out_shape=(
            jax.ShapeDtypeStruct(chunks.shape[1:], jnp.float32),
            jax.ShapeDtypeStruct(sums.shape, jnp.float32),
        ),
        in_specs=[vmem, vmem],
        out_specs=(vmem, vmem),
        scratch_shapes=[
            pltpu.VMEM((blks - 1,) + chunks.shape[1:], jnp.float32),
            pltpu.VMEM((owners - 1, part, lanes), jnp.float32),
            pltpu.VMEM((far, part, lanes), jnp.float32),
            pltpu.VMEM((DEPTH, part, lanes), jnp.float32),
            pltpu.VMEM(sums.shape, jnp.float32),
            dma((sends,)),
            dma((blks - 1,)),
            dma((owners - 1,)),
            dma((far - 1,)),
            dma((DEPTH - 1,)),
            dma((owners - 1,)),
        ],
        compiler_params=pltpu.CompilerParams(collective_id=0, has_side_effects=True, vmem_limit_bytes=4 << 20),
    )(chunks, sums)


def cut_kernel(list_ref, modes_ref, low_ref, high_ref):
    last = modes_ref.shape[2] - 1
    for n in range(2):
        rows = pl.ds(pl.multiple_of(list_ref[n, 1] * FBLK, FBLK), FBLK)
        low_ref[n] = modes_ref[:, :, 0, rows, :]
        high_ref[n] = modes_ref[:, :, last, rows, :]


def cut(block_list, modes):
    blocks, comps, _, _, lanes = modes.shape
    vmem = pl.BlockSpec(memory_space=pltpu.VMEM)
    side = jax.ShapeDtypeStruct((2, blocks, comps, FBLK, lanes), jnp.bfloat16)
    return pl.pallas_call(
        cut_kernel,
        out_shape=(side, side),
        in_specs=[pl.BlockSpec(memory_space=pltpu.SMEM), vmem],
        out_specs=(vmem, vmem),
        compiler_params=pltpu.CompilerParams(vmem_limit_bytes=8 << 20),
    )(block_list, modes)


def finish_kernel(scale_field, scale_triad, share_ref, whole_ref, transfer_ref, triad_ref):
    groups, planes = share_ref.shape[:2]
    for g in range(groups):
        for p in range(planes):
            transfer_ref[8 * g : 8 * g + 8, p, :] = share_ref[g, p] * scale_field
    for n in range(2):
        triad_ref[n] = whole_ref[:, n * FBLK : (n + 1) * FBLK] * scale_triad


def finish(share, whole, scale_field, scale_triad):
    groups, planes, rows, lanes = share.shape
    vmem = pl.BlockSpec(memory_space=pltpu.VMEM)
    return pl.pallas_call(
        functools.partial(finish_kernel, scale_field, scale_triad),
        out_shape=(
            jax.ShapeDtypeStruct((groups * rows, planes, lanes), jnp.float32),
            jax.ShapeDtypeStruct((2, FBLK, FBLK), jnp.float32),
        ),
        in_specs=[vmem, vmem],
        out_specs=(vmem, vmem),
        compiler_params=pltpu.CompilerParams(vmem_limit_bytes=4 << 20),
    )(share, whole)


def per_device(velocity_modes, block_list, counts):
    blocks_here, _, _, freq_count, planes, cross_cells = velocity_modes.shape
    welch_all = blocks_here * lax.axis_size("blk")
    cells_all = planes * lax.axis_size("cell") * cross_cells
    scale_field = -0.5 * 0.25 / math.sqrt(welch_all * FBLK)
    scale_triad = -0.5 * 0.25 / math.sqrt(welch_all * cells_all)

    modes = velocity_modes.reshape(blocks_here, 6, freq_count, planes, cross_cells).swapaxes(2, 3)
    low_planes, high_planes = cut(block_list, modes)
    grouped, packed, below, above = run_regroup(modes, low_planes, high_planes)
    field, sums = run_triads(block_list, counts, modes, below, above, grouped, packed)
    share, triads = exchange(field, sums)
    return finish(share, triads, scale_field, scale_triad)


def solution(mesh):
    return jax.shard_map(
        per_device,
        mesh=mesh,
        in_specs=(P("blk", None, None, None, "cell", None), P(), P()),
        out_specs=(P("blk", "cell", None), P()),
        check_vma=False,
    )
```

```python
import functools
import math

import jax
import jax.numpy as jnp
from jax import lax
from jax.experimental import pallas as pl
from jax.experimental.pallas import tpu as pltpu
from jax.sharding import PartitionSpec as P

FBLK = 64
CZ = 16
CORES = 2
DEPTH = 8


def slot_spread(parts):
    slot = lax.broadcasted_iota(jnp.int32, parts[0].shape, 1) // CZ
    for k in (1, 2, 4):
        odd = slot & k != 0
        parts = [jnp.where(odd, parts[(e + k) % 8], parts[e]) for e in range(8)]
    return [parts[-y % 8] for y in range(8)]


def slot_transpose(parts):
    width = parts[0].shape[1]
    turned = [parts[0]] + [pltpu.roll(parts[s], CZ * s, 1) for s in range(1, 8)]
    mixed = slot_spread(turned)
    return [mixed[0]] + [pltpu.roll(mixed[y], width - CZ * y, 1) for y in range(1, 8)]


def row_sums(parts):
    row = lax.broadcasted_iota(jnp.int32, parts[0].shape, 0)
    parts = list(parts)
    for k in (4, 2, 1):
        keep = row & k == 0
        merged = []
        for a in range(k):
            first, second = parts[a], parts[a + k]
            other = jnp.where(keep, second, first)
            if k == 4:
                other = pltpu.roll(other, 4, 0)
            else:
                other = jnp.where(keep, pltpu.roll(other, 8 - k, 0), pltpu.roll(other, k, 0))
            merged.append(jnp.where(keep, first, second) + other)
        parts = merged
    return parts[0]


def regroup_kernel(modes_ref, low_ref, high_ref, grouped, packed, below_ref, above_ref, sent, got):
    cells = lax.axis_size("cell")
    cell = lax.axis_index("cell")
    blk = lax.axis_index("blk")
    mesh_id = pl.DeviceIdType.MESH
    up = (lax.rem(cell + 1, cells), blk)
    down = (lax.rem(cell + cells - 1, cells), blk)
    barrier = pltpu.get_barrier_semaphore()
    for peer in (up, down):
        pl.semaphore_signal(barrier, inc=1, device_id=peer, device_id_type=mesh_id)
    pl.semaphore_wait(barrier, 2)
    copies = [
        pltpu.make_async_remote_copy(
            src_ref=source,
            dst_ref=target,
            send_sem=sent.at[k],
            recv_sem=got.at[k],
            device_id=peer,
            device_id_type=mesh_id,
        )
        for k, (source, target, peer) in enumerate([(high_ref, below_ref, up), (low_ref, above_ref, down)])
    ]
    for copy in copies:
        copy.start()

    def regroup(index, _):
        p = index % 4
        i = index // 4 % 3
        b = index // 12
        for block in range(4):
            parts = []
            for v in range(8):
                rows = pl.ds(block * FBLK + 8 * v, 8)
                parts.append(
                    jnp.concatenate(
                        [modes_ref[b, 2 * i, p, rows, :], modes_ref[b, 2 * i + 1, p, rows, :]], axis=0
                    )
                )
            parts = slot_transpose(parts)
            for y in range(8):
                packed[b, 8 * p + y, i, block] = parts[y]
                grouped[b, 8 * p + y, i, block] = parts[y].astype(jnp.float32)
        return 0

    lax.fori_loop(0, 24, regroup, 0)
    for copy in copies:
        copy.wait()

    @pl.when(cell == 0)
    def _():
        below_ref[...] = jnp.zeros_like(below_ref)

    @pl.when(cell == cells - 1)
    def _():
        above_ref[...] = jnp.zeros_like(above_ref)


def triad_kernel(
    list_ref,
    count_ref,
    modes_ref,
    below_ref,
    above_ref,
    grouped,
    packed,
    field_ref,
    sums_ref,
    left_a,
    left_b,
    right_a,
    right_b,
    window_a,
    window_b,
    pair_sums,
    rows_out,
    triads,
):
    lefts, rights, windows = (left_a, left_b), (right_a, right_b), (window_a, window_b)
    lanes = modes_ref.shape[4]
    field_ref[...] = jnp.zeros_like(field_ref)
    right_a[...] = jnp.zeros_like(right_a)
    right_b[...] = jnp.zeros_like(right_b)

    lane = lax.broadcasted_iota(jnp.int32, (16, lanes), 1)
    row = lax.broadcasted_iota(jnp.int32, (16, lanes), 0)
    z = lane % CZ
    slot = lane // CZ
    slot8 = lax.broadcasted_iota(jnp.int32, (8, lanes), 1) // CZ
    row8 = lax.broadcasted_iota(jnp.int32, (8, lanes), 0)
    picked = (slot8 == row8).astype(jnp.float32)
    zero = jnp.zeros((16, lanes), jnp.bfloat16)

    def fill_left(plane, index, left):
        n = plane // 4
        p = plane % 4
        at_l = list_ref[n, 1]
        cc = index % 4
        i = index // 4 % 3
        b = index // 12
        first = pl.multiple_of(at_l * FBLK + cc * 16, 16)
        own = pl.ds(pl.multiple_of(cc * 16, 16), 16)
        shifted = []
        for part in range(2):
            comp = 2 * i + part
            u = modes_ref[b, comp, p, pl.ds(first, 16), :]
            up = modes_ref[b, comp, jnp.minimum(p + 1, 3), pl.ds(first, 16), :]
            down = modes_ref[b, comp, jnp.maximum(p - 1, 0), pl.ds(first, 16), :]
            up = jnp.where(p == 3, above_ref[n, b, comp, own, :], up)
            down = jnp.where(p == 0, below_ref[n, b, comp, own, :], down)
            shifted.append(
                slot_spread(
                    [
                        up,
                        pltpu.roll(-down, CZ, 1),
                        jnp.where(slot == 1, zero, pltpu.roll(u, CZ, 1)),
                        jnp.where(slot == 3, zero, pltpu.roll(-u, 4 * CZ, 1)),
                        jnp.where(z == CZ - 1, zero, pltpu.roll(u, 4 * CZ - 1, 1)),
                        jnp.where(z == 0, zero, pltpu.roll(-u, 5 * CZ + 1, 1)),
                        zero,
                        zero,
                    ]
                )
            )
        at = pl.multiple_of((cc * 3 + i) * 32, 32)
        for y in range(8):
            real = shifted[0][y]
            imag = shifted[1][y]
            left[b, y, pl.ds(at, 16), :lanes] = real
            left[b, y, pl.ds(at, 16), lanes:] = -imag
            left[b, y, pl.ds(at + 16, 16), :lanes] = imag
            left[b, y, pl.ds(at + 16, 16), lanes:] = real

    def build(step, right, window):
        n = step // 32
        group = step % 32
        at_k = list_ref[n, 0]
        at_m = at_k + list_ref[n, 1]
        y = group % 8
        for b in range(2):
            for i in range(3):
                now = packed[b, group, i, at_m]
                later = packed[b, group, i, at_m + 1]
                for g in range(9):
                    turned = now if g == 0 else later
                    if 0 < g < 8:
                        turned = pltpu.roll(jnp.where(slot >= g, now, later), lanes - CZ * g, 1)
                    turned = turned.astype(jnp.float32)
                    for part in range(2):
                        window[b, 2 * i + part, 8 * g : 8 * g + 8, :] = turned[8 * part : 8 * part + 8]
                for part in range(2):
                    for a in range(8):
                        donor = grouped[b, group, i, at_k, pl.ds(8 * part + a, 16, stride=0), :]
                        spread = jnp.where(z == row, donor, 0.0).astype(jnp.bfloat16)
                        for side in range(2):
                            top = pl.multiple_of(part * lanes + (y + 2 * i + side) % 8 * 16, 16)
                            right[b, pl.ds(top, 16), a * lanes : (a + 1) * lanes] = spread

    def contract(y, live, left, right, window):
        kept_all = []
        for a2 in range(4):
            products = [
                jnp.dot(
                    left[b, y],
                    right[b, :, a2 * 2 * lanes : (a2 + 1) * 2 * lanes],
                    preferred_element_type=jnp.float32,
                )
                for b in range(2)
            ]
            for half in range(2):
                a = 2 * a2 + half
                kept = None
                for ch in range(FBLK // 8):
                    total = None
                    for b in range(2):
                        for comp in range(6):
                            at = (ch // 2 * 6 + comp) * 16 + 8 * (ch % 2)
                            term = (
                                products[b][at : at + 8, half * lanes : (half + 1) * lanes]
                                * window[b, comp, 8 * ch + a : 8 * ch + a + 8, :]
                            )
                            total = term if total is None else total + term
                    pair_sums[a, 8 * ch : 8 * ch + 8, :] += total
                    masked = jnp.where(row8 < live - 8 * ch, total, 0.0)
                    kept = masked if kept is None else kept + masked
                kept_all.append(kept)
        rows_out[y] = row_sums(kept_all)

    lax.fori_loop(0, 24, lambda index, _: (fill_left(0, index, left_a), 0)[1], 0, unroll=4)
    build(0, right_a, window_a)

    def plane_pair(t, _):
        n = t // 2
        at_k = list_ref[n, 0]
        live = count_ref[n]

        @pl.when(t % 2 == 0)
        def _():
            pair_sums[...] = jnp.zeros_like(pair_sums)

        for parity in range(2):
            plane = 2 * t + parity

            def group_pair(y2, _):
                for half in range(4):
                    y = 4 * y2 + half
                    contract(y, live, lefts[parity], rights[half % 2], windows[half % 2])
                    build(jnp.minimum(plane * 8 + y + 1, 63), rights[1 - half % 2], windows[1 - half % 2])
                    for piece in range(3):
                        fill_left(jnp.minimum(plane + 1, 7), 3 * y + piece, lefts[1 - parity])
                return 0

            lax.fori_loop(0, 2, group_pair, 0)
            parts = slot_transpose([rows_out[y] for y in range(8)])
            for v in range(8):
                field_ref[at_k * 8 + v, plane % 4] += parts[v]

        @pl.when(t % 2 == 1)
        def _():
            for a in range(8):
                triads[n, pl.ds(a, 8, stride=8), :] = lax.dot_general(
                    picked,
                    pair_sums[a],
                    (((1,), (1,)), ((), ())),
                    precision=lax.Precision.HIGHEST,
                    preferred_element_type=jnp.float32,
                )

        return 0

    lax.fori_loop(0, 4, plane_pair, 0)
    column = lax.broadcasted_iota(jnp.int32, (FBLK, FBLK), 1)
    for n in range(2):
        sums_ref[:, n * FBLK : (n + 1) * FBLK] = jnp.where(column < count_ref[n], triads[n], 0.0)


def run_regroup(modes, low_planes, high_planes):
    lanes = modes.shape[4]
    vmem = pl.BlockSpec(memory_space=pltpu.VMEM)
    shape = (2, 32, 3, 4, 16, lanes)
    side = jax.ShapeDtypeStruct(low_planes.shape, low_planes.dtype)
    return pl.pallas_call(
        regroup_kernel,
        out_shape=(jax.ShapeDtypeStruct(shape, jnp.float32), jax.ShapeDtypeStruct(shape, jnp.bfloat16), side, side),
        in_specs=[vmem] * 3,
        out_specs=(vmem,) * 4,
        scratch_shapes=[pltpu.SemaphoreType.DMA((2,)), pltpu.SemaphoreType.DMA((2,))],
        compiler_params=pltpu.CompilerParams(collective_id=1, has_side_effects=True, vmem_limit_bytes=16 << 20),
    )(modes, low_planes, high_planes)


def run_triads(block_list, counts, modes, below, above, grouped, packed):
    planes, freq_count, cross_cells = modes.shape[2:]
    donors_span = (freq_count // FBLK - 1) * FBLK
    vmem = pl.BlockSpec(memory_space=pltpu.VMEM)
    smem = pl.BlockSpec(memory_space=pltpu.SMEM)
    return pl.pallas_call(
        triad_kernel,
        out_shape=(
            jax.ShapeDtypeStruct((donors_span // 8, planes, 8, cross_cells), jnp.float32),
            jax.ShapeDtypeStruct((FBLK, 2 * FBLK), jnp.float32),
        ),
        in_specs=[smem, smem, vmem, vmem, vmem, vmem, vmem],
        out_specs=(vmem, vmem),
        scratch_shapes=[
            pltpu.VMEM((2, 8, 384, 2 * cross_cells), jnp.bfloat16),
            pltpu.VMEM((2, 8, 384, 2 * cross_cells), jnp.bfloat16),
            pltpu.VMEM((2, 2 * cross_cells, 8 * cross_cells), jnp.bfloat16),
            pltpu.VMEM((2, 2 * cross_cells, 8 * cross_cells), jnp.bfloat16),
            pltpu.VMEM((2, 6, 72, cross_cells), jnp.float32),
            pltpu.VMEM((2, 6, 72, cross_cells), jnp.float32),
            pltpu.VMEM((8, FBLK, cross_cells), jnp.float32),
            pltpu.VMEM((8, 8, cross_cells), jnp.float32),
            pltpu.VMEM((2, FBLK, FBLK), jnp.float32),
        ],
        compiler_params=pltpu.CompilerParams(vmem_limit_bytes=32 << 20),
    )(block_list, counts, modes, below, above, grouped, packed)


def exchange_kernel(
    field_ref,
    sums_ref,
    share_ref,
    whole_ref,
    field_in,
    part_in,
    x_in,
    z_in,
    whole,
    sent,
    field_got,
    part_got,
    x_got,
    z_got,
    whole_got,
):
    cell = lax.axis_index("cell")
    blk = lax.axis_index("blk")
    blks = field_ref.shape[0]
    owners = CORES * blks
    part = sums_ref.shape[0] // owners
    depth = z_in.shape[0]
    far = x_in.shape[0]
    near = depth * CORES
    core = lax.rem(cell, CORES)
    z_at = lax.rem(cell // CORES, depth)
    x_at = cell // near
    owner = blk * CORES + core
    mesh_id = pl.DeviceIdType.MESH

    def blk_peer(step):
        return (cell, lax.rem(blk + step, blks))

    def owner_peer(step):
        other = lax.rem(owner + step, owners)
        return (cell - core + lax.rem(other, CORES), other // CORES)

    def x_peer(step):
        return (lax.rem(x_at + step, far) * near + z_at * CORES + core, blk)

    def z_peer(step):
        return (x_at * near + lax.rem(z_at + step, depth) * CORES + core, blk)

    barrier = pltpu.get_barrier_semaphore()
    peers = [owner_peer(s) for s in range(1, owners)]
    peers += [x_peer(s) for s in range(1, far)]
    peers += [z_peer(s) for s in range(1, depth)]
    for peer in peers:
        pl.semaphore_signal(barrier, inc=1, device_id=peer, device_id_type=mesh_id)
    pl.semaphore_wait(barrier, len(peers))

    copies = []

    def send(source, target, got, peer):
        copy = pltpu.make_async_remote_copy(
            src_ref=source,
            dst_ref=target,
            send_sem=sent.at[len(copies)],
            recv_sem=got,
            device_id=peer,
            device_id_type=mesh_id,
        )
        copy.start()
        copies.append(copy)
        return copy

    def rows_of(at):
        return pl.ds(pl.multiple_of(at * part, part), part)

    first = []
    for s in range(1, owners):
        rows = rows_of(lax.rem(owner + s, owners))
        first.append(send(sums_ref.at[rows], part_in.at[s - 1], part_got.at[s - 1], owner_peer(s)))
    fields = []
    for s in range(1, blks):
        fields.append(
            send(field_ref.at[lax.rem(blk + s, blks)], field_in.at[s - 1], field_got.at[s - 1], blk_peer(s))
        )
    for copy in first:
        copy.wait_recv()
    total = sums_ref[rows_of(owner), :]
    for s in range(1, owners):
        total = total + part_in[s - 1]
    x_in[x_at] = total
    second = [send(x_in.at[x_at], x_in.at[x_at], x_got.at[s - 1], x_peer(s)) for s in range(1, far)]
    for copy in second:
        copy.wait_recv()
    total = x_in[0]
    for k in range(1, far):
        total = total + x_in[k]
    z_in[z_at] = total
    third = [send(z_in.at[z_at], z_in.at[z_at], z_got.at[s - 1], z_peer(s)) for s in range(1, depth)]
    for copy in third:
        copy.wait_recv()
    total = z_in[0]
    for k in range(1, depth):
        total = total + z_in[k]
    whole[rows_of(owner), :] = total
    fourth = [
        send(whole.at[rows_of(owner)], whole.at[rows_of(owner)], whole_got.at[s - 1], owner_peer(s))
        for s in range(1, owners)
    ]
    for copy in fields:
        copy.wait_recv()
    share = field_ref[blk]
    for s in range(1, blks):
        share = share + field_in[s - 1]
    share_ref[...] = share
    for copy in fourth:
        copy.wait_recv()
    whole_ref[...] = whole[...]
    for copy in copies:
        copy.wait_send()


def exchange(local_field, sums):
    blks = lax.axis_size("blk")
    owners = CORES * blks
    far = lax.axis_size("cell") // (DEPTH * CORES)
    share = local_field.shape[0] // blks
    chunks = local_field.reshape(blks, share, *local_field.shape[1:])
    part = sums.shape[0] // owners
    lanes = sums.shape[1]
    vmem = pl.BlockSpec(memory_space=pltpu.VMEM)
    dma = pltpu.SemaphoreType.DMA
    sends = 2 * (owners - 1) + (blks - 1) + (far - 1) + (DEPTH - 1)
    return pl.pallas_call(
        exchange_kernel,
        out_shape=(
            jax.ShapeDtypeStruct(chunks.shape[1:], jnp.float32),
            jax.ShapeDtypeStruct(sums.shape, jnp.float32),
        ),
        in_specs=[vmem, vmem],
        out_specs=(vmem, vmem),
        scratch_shapes=[
            pltpu.VMEM((blks - 1,) + chunks.shape[1:], jnp.float32),
            pltpu.VMEM((owners - 1, part, lanes), jnp.float32),
            pltpu.VMEM((far, part, lanes), jnp.float32),
            pltpu.VMEM((DEPTH, part, lanes), jnp.float32),
            pltpu.VMEM(sums.shape, jnp.float32),
            dma((sends,)),
            dma((blks - 1,)),
            dma((owners - 1,)),
            dma((far - 1,)),
            dma((DEPTH - 1,)),
            dma((owners - 1,)),
        ],
        compiler_params=pltpu.CompilerParams(collective_id=0, has_side_effects=True, vmem_limit_bytes=4 << 20),
    )(chunks, sums)


def cut_kernel(list_ref, modes_ref, low_ref, high_ref):
    last = modes_ref.shape[2] - 1
    for n in range(2):
        rows = pl.ds(pl.multiple_of(list_ref[n, 1] * FBLK, FBLK), FBLK)
        low_ref[n] = modes_ref[:, :, 0, rows, :]
        high_ref[n] = modes_ref[:, :, last, rows, :]


def cut(block_list, modes):
    blocks, comps, _, _, lanes = modes.shape
    vmem = pl.BlockSpec(memory_space=pltpu.VMEM)
    side = jax.ShapeDtypeStruct((2, blocks, comps, FBLK, lanes), jnp.bfloat16)
    return pl.pallas_call(
        cut_kernel,
        out_shape=(side, side),
        in_specs=[pl.BlockSpec(memory_space=pltpu.SMEM), vmem],
        out_specs=(vmem, vmem),
        compiler_params=pltpu.CompilerParams(vmem_limit_bytes=8 << 20),
    )(block_list, modes)


def finish_kernel(scale_field, scale_triad, share_ref, whole_ref, transfer_ref, triad_ref):
    groups, planes = share_ref.shape[:2]
    for g in range(groups):
        for p in range(planes):
            transfer_ref[8 * g : 8 * g + 8, p, :] = share_ref[g, p] * scale_field
    for n in range(2):
        triad_ref[n] = whole_ref[:, n * FBLK : (n + 1) * FBLK] * scale_triad


def finish(share, whole, scale_field, scale_triad):
    groups, planes, rows, lanes = share.shape
    vmem = pl.BlockSpec(memory_space=pltpu.VMEM)
    return pl.pallas_call(
        functools.partial(finish_kernel, scale_field, scale_triad),
        out_shape=(
            jax.ShapeDtypeStruct((groups * rows, planes, lanes), jnp.float32),
            jax.ShapeDtypeStruct((2, FBLK, FBLK), jnp.float32),
        ),
        in_specs=[vmem, vmem],
        out_specs=(vmem, vmem),
        compiler_params=pltpu.CompilerParams(vmem_limit_bytes=4 << 20),
    )(share, whole)


def per_device(velocity_modes, block_list, counts):
    blocks_here, _, _, freq_count, planes, cross_cells = velocity_modes.shape
    welch_all = blocks_here * lax.axis_size("blk")
    cells_all = planes * lax.axis_size("cell") * cross_cells
    scale_field = -0.5 * 0.25 / math.sqrt(welch_all * FBLK)
    scale_triad = -0.5 * 0.25 / math.sqrt(welch_all * cells_all)

    modes = velocity_modes.reshape(blocks_here, 6, freq_count, planes, cross_cells).swapaxes(2, 3)
    low_planes, high_planes = cut(block_list, modes)
    grouped, packed, below, above = run_regroup(modes, low_planes, high_planes)
    field, sums = run_triads(block_list, counts, modes, below, above, grouped, packed)
    share, triads = exchange(field, sums)
    return finish(share, triads, scale_field, scale_triad)


def solution(mesh):
    return jax.shard_map(
        per_device,
        mesh=mesh,
        in_specs=(P("blk", None, None, None, "cell", None), P(), P()),
        out_specs=(P("blk", "cell", None), P()),
        check_vma=False,
    )
```
